512 devices in a mesh: lat: 16 (over y, x_lo, core), lon: 32 (over z, x_hi).
Axes of the slice: x: 4 (x_hi: 2, x_lo: 2; x = x_hi * 2 + x_lo), y: 4, z: 16, core: 2. Of those that a mesh axis runs over, the one named last changes fastest.
Arguments:
- queries: bfloat16 [384, 768, 128], P('lat', 'lon'), may hold values from -8 to 8
- keys: bfloat16 [384, 768, 128], P('lat', 'lon'), may hold values from -8 to 8
- values: bfloat16 [384, 768, 128], P('lat', 'lon'), may hold values from -6 to 6
- out_grad: bfloat16 [384, 768, 128], P('lat', 'lon'), may hold values from -6 to 6
Outputs:
- attended: bfloat16 [384, 768, 128], P('lat', 'lon')
- grad_queries: bfloat16 [384, 768, 128], P('lat', 'lon')
- grad_keys: bfloat16 [384, 768, 128], P('lat', 'lon')
- grad_values: bfloat16 [384, 768, 128], P('lat', 'lon')
The draws below stay inside these ranges and needn't reach their ends.
All inputs are finite; a program needn't handle non-finite values.
Results may differ from the reference program's by a relative error of at most 0.018.
Values may be sent and summed in bfloat16 or wider, within the bound.
No kernel may reach another device: no remote copies, remote signals or barrier semaphores. Data moves between devices by JAX's collectives and lax.ppermute only.
A program may use at most 128 MiB of HBM per device.

```python
import math
import jax
import jax.numpy as jnp
from jax import lax

HEADS = 2
HEAD_DIM = 64
RADIUS = 22
BLOCK_LAT = 8
BLOCK_LON = 24
WINDOW = 45
CHANNELS = 128
LAT_CELLS = 384
LON_CELLS = 768


def draw_queries(key, part):
    shape = (LAT_CELLS, LON_CELLS, CHANNELS)
    return jnp.clip(jax.random.normal(jax.random.fold_in(key, 21), shape, jnp.float32), -6.0, 6.0).astype(jnp.bfloat16)


def draw_keys(key, part):
    shape = (LAT_CELLS, LON_CELLS, CHANNELS)
    return jnp.clip(jax.random.normal(jax.random.fold_in(key, 22), shape, jnp.float32), -6.0, 6.0).astype(jnp.bfloat16)


def block_scale(stream_key, extent, split, least, largest):
    def one(position, parts):
        draws = jax.random.uniform(jax.random.fold_in(jax.random.fold_in(stream_key, 6), position), (parts,), jnp.float32, least / len(split), largest / len(split))
        return jnp.repeat(jnp.exp(draws), extent[position] // parts).reshape((-1,) + (1,) * (len(extent) - position - 1))

    loudness = one(*split[0])
    for cut in split[1:]:
        loudness = loudness * one(*cut)
    return loudness


def normal_values(key, dims, scale, bound, split=(), kind=jnp.bfloat16):
    factor_of = block_scale(key, dims, split, -0.22, 0.18) if split else 1.0
    array = jax.random.normal(key, dims, jnp.float32) * scale * factor_of
    return jnp.minimum(jnp.maximum(array, -bound), bound).astype(kind)


def setup_inputs(seed: int = 0) -> dict:
    streams_of = jax.random.split(jax.random.key(seed), 5)
    return {
        "queries": draw_queries(jax.random.fold_in(streams_of[4], 71), 0),
        "keys": draw_keys(jax.random.fold_in(streams_of[4], 71), 0),
        "values": normal_values(streams_of[2], (LAT_CELLS, LON_CELLS, CHANNELS), 1.0, 6.0, ((0, 16), (1, 32))),
        "out_grad": normal_values(streams_of[3], (LAT_CELLS, LON_CELLS, CHANNELS), 1.0, 6.0, ((0, 16), (1, 32))),
    }


masked_value = -1e+30

def window_mask(query_rows, key_rows, height):
    first_key = jnp.clip(query_rows - RADIUS, 0, height - WINDOW)
    lat_ok = (key_rows[None, :] >= first_key[:, None]) & (key_rows[None, :] < first_key[:, None] + WINDOW)
    offsets = jnp.arange(BLOCK_LON + 2 * RADIUS, dtype=jnp.int32)[None, :] - jnp.arange(BLOCK_LON, dtype=jnp.int32)[:, None]
    lon_ok = (offsets >= 0) & (offsets <= 2 * RADIUS)
    inside = lat_ok[:, None, :, None] & lon_ok[None, :, None, :]
    return inside.reshape(BLOCK_LAT * BLOCK_LON, (BLOCK_LAT + 2 * RADIUS) * (BLOCK_LON + 2 * RADIUS))

def attend(query_block, grad_block, key_slab, inside):
    query_count = query_block.shape[0]
    key_count = key_slab.shape[0]
    channels = query_block.shape[1]
    scale = 1.0 / math.sqrt(HEAD_DIM)
    query_heads = query_block.astype(jnp.float32).reshape(query_count, HEADS, HEAD_DIM)
    grad_heads = grad_block.astype(jnp.float32).reshape(query_count, HEADS, HEAD_DIM)
    key_heads = key_slab[:, :channels].astype(jnp.float32).reshape(key_count, HEADS, HEAD_DIM)
    value_heads = key_slab[:, channels:].astype(jnp.float32).reshape(key_count, HEADS, HEAD_DIM)
    scores = jnp.einsum('qhd,khd->hqk', query_heads, key_heads) * scale
    scores = jnp.where(inside[None], scores, masked_value)
    row_max = lax.optimization_barrier(jnp.max(scores, axis=-1))
    log_total = row_max + jnp.log(lax.optimization_barrier(jnp.sum(jnp.exp(scores - row_max[..., None]), axis=-1)))
    weights = lax.optimization_barrier(jnp.exp(scores - log_total[..., None]).astype(jnp.bfloat16)).astype(jnp.float32)
    attended = jnp.einsum('hqk,khd->qhd', weights, value_heads).astype(jnp.bfloat16)
    attended_wide = lax.optimization_barrier(attended).astype(jnp.float32)
    correction = lax.optimization_barrier(jnp.sum(grad_heads * attended_wide, axis=-1)).T
    grad_weights = jnp.einsum('qhd,khd->hqk', grad_heads, value_heads)
    grad_scores = (weights * (grad_weights - correction[..., None]) * scale).astype(jnp.bfloat16)
    grad_scores = lax.optimization_barrier(grad_scores).astype(jnp.float32)
    grad_query = jnp.einsum('hqk,khd->qhd', grad_scores, key_heads).astype(jnp.bfloat16)
    grad_key = jnp.einsum('hqk,qhd->khd', grad_scores, query_heads).reshape(key_count, channels)
    grad_value = jnp.einsum('hqk,qhd->khd', weights, grad_heads).reshape(key_count, channels)
    return (attended.reshape(query_count, channels), grad_query.reshape(query_count, channels), jnp.concatenate([grad_key, grad_value], axis=-1))

def reference(queries, keys, values, out_grad):
    height, width, channels = queries.shape
    key_value = jnp.concatenate([keys, values], axis=-1)
    key_value = jnp.concatenate([key_value[:, width - RADIUS:], key_value, key_value[:, :RADIUS]], axis=1)
    key_value = jnp.pad(key_value, ((RADIUS, RADIUS), (0, 0), (0, 0)))
    blocks_lat = height // BLOCK_LAT
    blocks_lon = width // BLOCK_LON
    slab_rows = BLOCK_LAT + 2 * RADIUS
    slab_cols = BLOCK_LON + 2 * RADIUS
    zero_index = jnp.zeros((), jnp.int32)

    def step(gradient, block_index):
        row_start = (block_index // blocks_lon * BLOCK_LAT).astype(jnp.int32)
        col_start = (block_index % blocks_lon * BLOCK_LON).astype(jnp.int32)
        first_key = jnp.clip(row_start - RADIUS, 0, height - WINDOW)
        slab_start = jnp.clip(first_key + RADIUS, 0, height - BLOCK_LAT).astype(jnp.int32)
        key_slab = lax.dynamic_slice(key_value, (slab_start, col_start, zero_index), (slab_rows, slab_cols, 2 * channels))
        key_slab = key_slab.reshape(slab_rows * slab_cols, 2 * channels)
        query_block = lax.dynamic_slice(queries, (row_start, col_start, zero_index), (BLOCK_LAT, BLOCK_LON, channels)).reshape(-1, channels)
        grad_block = lax.dynamic_slice(out_grad, (row_start, col_start, zero_index), (BLOCK_LAT, BLOCK_LON, channels)).reshape(-1, channels)
        query_rows = row_start + jnp.arange(BLOCK_LAT, dtype=jnp.int32)
        key_rows = slab_start - RADIUS + jnp.arange(slab_rows, dtype=jnp.int32)
        inside = window_mask(query_rows, key_rows, height)
        attended, grad_query, grad_pair = attend(query_block, grad_block, key_slab, inside)
        current = lax.dynamic_slice(gradient, (slab_start, col_start, zero_index), (slab_rows, slab_cols, 2 * channels))
        gradient = lax.dynamic_update_slice(gradient, current + grad_pair.reshape(slab_rows, slab_cols, 2 * channels), (slab_start, col_start, zero_index))
        return (gradient, (attended, grad_query))
    start_grad = jnp.zeros((height + 2 * RADIUS, width + 2 * RADIUS, 2 * channels), jnp.float32)
    gradient, stacked = lax.scan(step, start_grad, jnp.arange(blocks_lat * blocks_lon, dtype=jnp.int32))

    def assemble(pieces):
        shaped = pieces.reshape(blocks_lat, blocks_lon, BLOCK_LAT, BLOCK_LON, channels)
        return shaped.transpose(0, 2, 1, 3, 4).reshape(height, width, channels)
    cropped = gradient[RADIUS:height + RADIUS]
    interior = cropped[:, RADIUS:width + RADIUS]
    interior = interior.at[:, :RADIUS].add(cropped[:, width + RADIUS:])
    interior = interior.at[:, width - RADIUS:].add(cropped[:, :RADIUS])
    grad_keys = interior[..., :channels].astype(jnp.bfloat16)
    grad_values = interior[..., channels:].astype(jnp.bfloat16)
    return (assemble(stacked[0]), assemble(stacked[1]), grad_keys, grad_values)
```

```python
import jax
import jax.numpy as jnp
from jax import lax
from jax.experimental import pallas as pl
from jax.experimental.pallas import tpu as pltpu
from jax.sharding import PartitionSpec as P

R = 22
T = 24
W = 3 * T
ROWS = T + 2 * R
BR = 8
NB = T // BR
SR = BR + 2 * R
NK = SR * W
NQ = 2 * BR * T
KR = 4
CK = KR * W
NC = SR // KR
F32 = jnp.float32
BF = jnp.bfloat16
NT = (((1,), (1,)), ((), ()))
TN = (((0,), (0,)), ((), ()))


def kernel_a(start, k_ref, aux_ref, q_ref, g_ref, p_ref, linv_ref, gs_ref, vn_ref, vm_ref, vs_ref, s_scr, acc):
    b = pl.program_id(0)
    base = pl.multiple_of(start[b] * W, 64)

    @pl.when(b == 0)
    def _():
        acc[...] = jnp.zeros_like(acc)

    q = q_ref[0]

    def scores(c, m):
        at = pl.multiple_of(base + c * CK, 32)
        lhs = jnp.concatenate([k_ref[pl.ds(at, CK), :], aux_ref[pl.ds(at, CK), :]], axis=1)
        s = lax.dot_general(lhs, q, NT, preferred_element_type=F32)
        s_scr[pl.ds(pl.multiple_of(c * CK, 32), CK), :] = s
        return jnp.maximum(m, jnp.max(s.reshape(CK // 8, 8, NQ), axis=0))

    m = lax.fori_loop(0, NC, scores, jnp.full((8, NQ), -3e38, F32))
    m = jnp.max(m, axis=0, keepdims=True)

    def expo(c, l):
        at = pl.multiple_of(c * CK, 32)
        p = jnp.exp(s_scr[pl.ds(at, CK), :] - m)
        p_ref[0, pl.ds(at, CK), :] = p.astype(BF)
        return l + jnp.sum(p.reshape(CK // 8, 8, NQ), axis=0)

    l = lax.fori_loop(0, NC, expo, jnp.zeros((8, NQ), F32))
    linv = 1.0 / jnp.sum(l, axis=0, keepdims=True)
    linv_ref[0] = jnp.broadcast_to(linv, (8, NQ))
    turned = jnp.transpose(jnp.broadcast_to(linv, (128, NQ)))
    gs = (g_ref[0].astype(F32) * turned).astype(BF)
    gs_ref[0] = gs

    def dv(c, _):
        at = pl.multiple_of(base + c * CK, 32)
        p = p_ref[0, pl.ds(pl.multiple_of(c * CK, 32), CK), :]
        acc[pl.ds(at, CK), :] += jnp.dot(p, gs, preferred_element_type=F32)
        return 0

    lax.fori_loop(0, NC, dv, 0)

    @pl.when(b == NB - 1)
    def _():
        vn_ref[...] = acc[: R * W, :].astype(BF)
        vm_ref[...] = acc[R * W : (R + T) * W, :]
        vs_ref[...] = acc[(R + T) * W :, :].astype(BF)


def kernel_b(start, k_ref, v_ref, q_ref, gs_ref, p_ref, linv_ref, o_ref, dq_ref, kn_ref, km_ref, ks_ref, ot, acc):
    b = pl.program_id(0)
    base = pl.multiple_of(start[b] * W, 64)

    @pl.when(b == 0)
    def _():
        acc[...] = jnp.zeros_like(acc)

    q = q_ref[0][:, :128]
    gs = gs_ref[0]
    ot[...] = jnp.zeros_like(ot)

    def attend(c, _):
        at = pl.multiple_of(base + c * CK, 32)
        p = p_ref[0, pl.ds(pl.multiple_of(c * CK, 32), CK), :]
        ot[...] += lax.dot_general(v_ref[pl.ds(at, CK), :], p, TN, preferred_element_type=F32)
        return 0

    lax.fori_loop(0, NC, attend, 0)
    lane = lax.broadcasted_iota(jnp.int32, (NQ // 2, 128), 1)
    o = jnp.transpose(ot[...] * linv_ref[0][:1])
    o_bf = o.astype(BF)
    o_ref[...] = jnp.where(lane < 64, o[: NQ // 2], o[NQ // 2 :]).astype(BF)
    row = jnp.sum(gs.astype(F32) * o_bf.astype(F32), axis=1, keepdims=True)
    corr = jnp.transpose(jnp.broadcast_to(row, (NQ, 128)))[:1]
    ot[...] = jnp.zeros_like(ot)

    def back(c, _):
        at = pl.multiple_of(base + c * CK, 32)
        p = p_ref[0, pl.ds(pl.multiple_of(c * CK, 32), CK), :]
        gw = lax.dot_general(v_ref[pl.ds(at, CK), :], gs, NT, preferred_element_type=F32)
        ds = (p.astype(F32) * (gw - corr)).astype(BF)
        acc[pl.ds(at, CK), :] += jnp.dot(ds, q, preferred_element_type=F32)
        ot[...] += lax.dot_general(k_ref[pl.ds(at, CK), :], ds, TN, preferred_element_type=F32)
        return 0

    lax.fori_loop(0, NC, back, 0)
    dq = jnp.transpose(ot[...] * 0.125)
    dq_ref[...] = jnp.where(lane < 64, dq[: NQ // 2], dq[NQ // 2 :]).astype(BF)

    @pl.when(b == NB - 1)
    def _():
        kn_ref[...] = acc[: R * W, :].astype(BF)
        km_ref[...] = acc[R * W : (R + T) * W, :]
        ks_ref[...] = acc[(R + T) * W :, :].astype(BF)


def whole(shape):
    return pl.BlockSpec(shape, lambda b, s: (0,) * len(shape))


def per_block(shape):
    return pl.BlockSpec((1,) + shape, lambda b, s: (b,) + (0,) * len(shape))


def sds(shape, dtype):
    return jax.ShapeDtypeStruct(shape, dtype)


grads_shape = [sds((R * W, 128), BF), sds((T * W, 128), F32), sds((R * W, 128), BF)]
grads_spec = [whole((R * W, 128)), whole((T * W, 128)), whole((R * W, 128))]


def run_a(start, k, aux, q, g):
    return pl.pallas_call(
        kernel_a,
        grid_spec=pltpu.PrefetchScalarGridSpec(
            num_scalar_prefetch=1,
            grid=(NB,),
            in_specs=[whole((ROWS * W, 128)), whole((ROWS * W, 128)), per_block((NQ, 256)), per_block((NQ, 128))],
            out_specs=[per_block((NK, NQ)), per_block((8, NQ)), per_block((NQ, 128))] + grads_spec,
            scratch_shapes=[pltpu.VMEM((NK, NQ), F32), pltpu.VMEM((ROWS * W, 128), F32)],
        ),
        out_shape=[sds((NB, NK, NQ), BF), sds((NB, 8, NQ), F32), sds((NB, NQ, 128), BF)] + grads_shape,
        compiler_params=pltpu.CompilerParams(vmem_limit_bytes=48 << 20),
        cost_estimate=pl.CostEstimate(flops=6_000_000_000, bytes_accessed=14_000_000, transcendentals=4_000_000),
        name="scores_and_dv",
    )(start, k, aux, q, g)


def run_b(start, k, v, q, gs, p, linv):
    return pl.pallas_call(
        kernel_b,
        grid_spec=pltpu.PrefetchScalarGridSpec(
            num_scalar_prefetch=1,
            grid=(NB,),
            in_specs=[whole((ROWS * W, 128)), whole((ROWS * W, 128)), per_block((NQ, 256)), per_block((NQ, 128)), per_block((NK, NQ)), per_block((8, NQ))],
            out_specs=[pl.BlockSpec((NQ // 2, 128), lambda b, s: (b, 0)), pl.BlockSpec((NQ // 2, 128), lambda b, s: (b, 0))] + grads_spec,
            scratch_shapes=[pltpu.VMEM((128, NQ), F32), pltpu.VMEM((ROWS * W, 128), F32)],
        ),
        out_shape=[sds((T * T, 128), BF), sds((T * T, 128), BF)] + grads_shape,
        compiler_params=pltpu.CompilerParams(vmem_limit_bytes=48 << 20),
        cost_estimate=pl.CostEstimate(flops=8_000_000_000, bytes_accessed=14_000_000, transcendentals=0),
        name="attended_and_dk",
    )(start, k, v, q, gs, p, linv)


def tables(first_row, height):
    i0 = first_row + BR * jnp.arange(NB, dtype=jnp.int32)
    f0 = jnp.clip(i0 - R, 0, height - 45)
    start = jnp.clip(f0 - first_row + R, 0, ROWS - SR) // 8 * 8
    krow = lax.broadcasted_iota(jnp.int32, (ROWS, W, 128), 0) + (first_row - R)
    kcol = lax.broadcasted_iota(jnp.int32, (ROWS, W, 128), 1)
    lane = lax.broadcasted_iota(jnp.int32, (ROWS, W, 128), 2)
    f = jnp.clip(first_row + lane - R, 0, height - 45)
    row_out = (lane < T) & ((krow < f) | (krow >= f + 45))
    qcol = lane - T
    col_out = (lane >= T) & (lane < 2 * T) & ((kcol < qcol + 2) | (kcol > qcol + 46))
    aux = jnp.where(row_out | col_out, -1e30, 0.0).astype(BF).reshape(ROWS * W, 128)
    return start.astype(jnp.int32), aux


def spread(x, scale):
    x = (x.reshape(NB, 1, BR * T, 128) * scale).astype(BF)
    lane = lax.broadcasted_iota(jnp.int32, (1, 2, 1, 128), 3) // 64
    head = lax.broadcasted_iota(jnp.int32, (1, 2, 1, 128), 1)
    return jnp.where(lane == head, x, jnp.zeros((), BF)).reshape(NB, NQ, 128)


def with_marks(q):
    lane = lax.broadcasted_iota(jnp.int32, (NB, 2, BR, T, 128), 4)
    row = lax.broadcasted_iota(jnp.int32, (NB, 2, BR, T, 128), 0) * BR + lax.broadcasted_iota(jnp.int32, (NB, 2, BR, T, 128), 2)
    col = lax.broadcasted_iota(jnp.int32, (NB, 2, BR, T, 128), 3)
    mark = jnp.where((lane == row) | (lane == T + col), 1.0, 0.0).astype(BF).reshape(NB, NQ, 128)
    return jnp.concatenate([spread(q, 0.125), mark], axis=2)


def shift(x, axis, by, closed):
    n = lax.axis_size(axis)
    pairs = [(i, (i + by) % n) for i in range(n) if closed or 0 <= i + by < n]
    return lax.ppermute(x, axis, pairs)


def extend(x):
    mid = jnp.concatenate([shift(x, "lon", 1, True), x, shift(x, "lon", -1, True)], axis=1)
    north = shift(mid[T - R :], "lat", 1, False)
    south = shift(mid[:R], "lat", -1, False)
    return jnp.concatenate([north, mid, south], axis=0).reshape(ROWS * W, 128)


def fold(north, mid, south):
    north = north.reshape(R, W, 128)
    south = south.reshape(R, W, 128)
    from_south = shift(north, "lat", -1, False).astype(F32)
    from_north = shift(south, "lat", 1, False).astype(F32)
    pad = ((T - R, 0), (0, 0), (0, 0)), ((0, T - R), (0, 0), (0, 0))
    mid = mid.reshape(T, W, 128) + jnp.pad(from_south, pad[0]) + jnp.pad(from_north, pad[1])
    from_east = shift(mid[:, :T].astype(BF), "lon", -1, True).astype(F32)
    from_west = shift(mid[:, 2 * T :].astype(BF), "lon", 1, True).astype(F32)
    return (mid[:, T : 2 * T] + from_east + from_west).astype(BF)


def body(queries, keys, values, out_grad):
    height = T * lax.axis_size("lat")
    start, aux = tables(lax.axis_index("lat") * T, height)
    q = with_marks(queries)
    g = spread(out_grad, 1.0)
    k = extend(keys)
    v = extend(values)
    p, linv, gs, *dv = run_a(start, k, aux, q, g)
    grad_values = fold(*dv)
    attended, grad_queries, *dk = run_b(start, k, v, q, gs, p, linv)
    grad_keys = fold(*dk)
    return attended.reshape(T, T, 128), grad_queries.reshape(T, T, 128), grad_keys, grad_values


def solution(mesh):
    spec = P("lat", "lon", None)
    return jax.shard_map(body, mesh=mesh, in_specs=(spec,) * 4, out_specs=(spec,) * 4, check_vma=False)
```

```python
import jax
import jax.numpy as jnp
from jax import lax
from jax.experimental import pallas as pl
from jax.experimental.pallas import tpu as pltpu
from jax.sharding import PartitionSpec as P

R = 22
T = 24
W = 3 * T
ROWS = T + 2 * R
BR = 8
NB = T // BR
SR = BR + 2 * R
NK = SR * W
NQ = 2 * BR * T
CA = SR * W // 2
CB = SR * W
F32 = jnp.float32
BF = jnp.bfloat16
NT = (((1,), (1,)), ((), ()))
TN = (((0,), (0,)), ((), ()))


def kernel_a(start, k_ref, aux_ref, q_ref, g_ref, p_ref, linv_ref, gs_ref, vn_ref, vm_ref, vs_ref, s_scr, acc):
    b = pl.program_id(0)
    base = pl.multiple_of(start[b] * W, 64)

    @pl.when(b == 0)
    def _():
        acc[...] = jnp.zeros_like(acc)

    q = q_ref[0]

    def scores(c, m):
        at = pl.multiple_of(base + c * CA, 32)
        lhs = jnp.concatenate([k_ref[pl.ds(at, CA), :], aux_ref[pl.ds(at, CA), :]], axis=1)
        s = lax.dot_general(lhs, q, NT, preferred_element_type=F32)
        s_scr[pl.ds(pl.multiple_of(c * CA, 32), CA), :] = s
        return jnp.maximum(m, jnp.max(s.reshape(CA // 8, 8, NQ), axis=0))

    m = lax.fori_loop(0, NK // CA, scores, jnp.full((8, NQ), -3e38, F32))
    m = jnp.max(m, axis=0, keepdims=True)

    def expo(c, l):
        at = pl.multiple_of(c * CA, 32)
        p = jnp.exp(s_scr[pl.ds(at, CA), :] - m)
        p_ref[0, pl.ds(at, CA), :] = p.astype(BF)
        return l + jnp.sum(p.reshape(CA // 8, 8, NQ), axis=0)

    l = lax.fori_loop(0, NK // CA, expo, jnp.zeros((8, NQ), F32))
    linv = 1.0 / jnp.sum(l, axis=0, keepdims=True)
    linv_ref[0] = jnp.broadcast_to(linv, (8, NQ))
    turned = jnp.transpose(jnp.broadcast_to(linv, (128, NQ)))
    gs = (g_ref[0].astype(F32) * turned).astype(BF)
    gs_ref[0] = gs

    def dv(c, _):
        at = pl.multiple_of(base + c * CA, 32)
        p = p_ref[0, pl.ds(pl.multiple_of(c * CA, 32), CA), :]
        acc[pl.ds(at, CA), :] += jnp.dot(p, gs, preferred_element_type=F32)
        return 0

    lax.fori_loop(0, NK // CA, dv, 0)

    @pl.when(b == NB - 1)
    def _():
        vn_ref[...] = acc[: R * W, :].astype(BF)
        vm_ref[...] = acc[R * W : (R + T) * W, :]
        vs_ref[...] = acc[(R + T) * W :, :].astype(BF)


def kernel_b(start, k_ref, v_ref, q_ref, gs_ref, p_ref, linv_ref, o_ref, dq_ref, kn_ref, km_ref, ks_ref, ot, acc):
    b = pl.program_id(0)
    base = pl.multiple_of(start[b] * W, 64)

    @pl.when(b == 0)
    def _():
        acc[...] = jnp.zeros_like(acc)

    q = q_ref[0][:, :128]
    gs = gs_ref[0]
    ot[...] = jnp.zeros_like(ot)

    def attend(c, _):
        at = pl.multiple_of(base + c * CB, 32)
        p = p_ref[0, pl.ds(pl.multiple_of(c * CB, 32), CB), :]
        ot[...] += lax.dot_general(v_ref[pl.ds(at, CB), :], p, TN, preferred_element_type=F32)
        return 0

    lax.fori_loop(0, NK // CB, attend, 0)
    lane = lax.broadcasted_iota(jnp.int32, (NQ // 2, 128), 1)
    o = jnp.transpose(ot[...] * linv_ref[0][:1])
    o_bf = o.astype(BF)
    o_ref[...] = jnp.where(lane < 64, o[: NQ // 2], o[NQ // 2 :]).astype(BF)
    row = jnp.sum(gs.astype(F32) * o_bf.astype(F32), axis=1, keepdims=True)
    corr = jnp.transpose(jnp.broadcast_to(row, (NQ, 128)))[:1]
    ot[...] = jnp.zeros_like(ot)

    def back(c, _):
        at = pl.multiple_of(base + c * CB, 32)
        p = p_ref[0, pl.ds(pl.multiple_of(c * CB, 32), CB), :]
        gw = lax.dot_general(v_ref[pl.ds(at, CB), :], gs, NT, preferred_element_type=F32)
        ds = (p.astype(F32) * (gw - corr)).astype(BF)
        acc[pl.ds(at, CB), :] += jnp.dot(ds, q, preferred_element_type=F32)
        ot[...] += lax.dot_general(k_ref[pl.ds(at, CB), :], ds, TN, preferred_element_type=F32)
        return 0

    lax.fori_loop(0, NK // CB, back, 0)
    dq = jnp.transpose(ot[...] * 0.125)
    dq_ref[...] = jnp.where(lane < 64, dq[: NQ // 2], dq[NQ // 2 :]).astype(BF)

    @pl.when(b == NB - 1)
    def _():
        kn_ref[...] = acc[: R * W, :].astype(BF)
        km_ref[...] = acc[R * W : (R + T) * W, :]
        ks_ref[...] = acc[(R + T) * W :, :].astype(BF)


def whole(shape):
    return pl.BlockSpec(shape, lambda b, s: (0,) * len(shape))


def per_block(shape):
    return pl.BlockSpec((1,) + shape, lambda b, s: (b,) + (0,) * len(shape))


def sds(shape, dtype):
    return jax.ShapeDtypeStruct(shape, dtype)


grads_shape = [sds((R * W, 128), BF), sds((T * W, 128), F32), sds((R * W, 128), BF)]
grads_spec = [whole((R * W, 128)), whole((T * W, 128)), whole((R * W, 128))]


def run_a(start, k, aux, q, g):
    return pl.pallas_call(
        kernel_a,
        grid_spec=pltpu.PrefetchScalarGridSpec(
            num_scalar_prefetch=1,
            grid=(NB,),
            in_specs=[whole((ROWS * W, 128)), whole((ROWS * W, 128)), per_block((NQ, 256)), per_block((NQ, 128))],
            out_specs=[per_block((NK, NQ)), per_block((8, NQ)), per_block((NQ, 128))] + grads_spec,
            scratch_shapes=[pltpu.VMEM((NK, NQ), F32), pltpu.VMEM((ROWS * W, 128), F32)],
        ),
        out_shape=[sds((NB, NK, NQ), BF), sds((NB, 8, NQ), F32), sds((NB, NQ, 128), BF)] + grads_shape,
        compiler_params=pltpu.CompilerParams(vmem_limit_bytes=48 << 20),
        cost_estimate=pl.CostEstimate(flops=6_000_000_000, bytes_accessed=14_000_000, transcendentals=4_000_000),
        name="scores_and_dv",
    )(start, k, aux, q, g)


def run_b(start, k, v, q, gs, p, linv):
    return pl.pallas_call(
        kernel_b,
        grid_spec=pltpu.PrefetchScalarGridSpec(
            num_scalar_prefetch=1,
            grid=(NB,),
            in_specs=[whole((ROWS * W, 128)), whole((ROWS * W, 128)), per_block((NQ, 256)), per_block((NQ, 128)), per_block((NK, NQ)), per_block((8, NQ))],
            out_specs=[pl.BlockSpec((NQ // 2, 128), lambda b, s: (b, 0)), pl.BlockSpec((NQ // 2, 128), lambda b, s: (b, 0))] + grads_spec,
            scratch_shapes=[pltpu.VMEM((128, NQ), F32), pltpu.VMEM((ROWS * W, 128), F32)],
        ),
        out_shape=[sds((T * T, 128), BF), sds((T * T, 128), BF)] + grads_shape,
        compiler_params=pltpu.CompilerParams(vmem_limit_bytes=48 << 20),
        cost_estimate=pl.CostEstimate(flops=8_000_000_000, bytes_accessed=14_000_000, transcendentals=0),
        name="attended_and_dk",
    )(start, k, v, q, gs, p, linv)


def tables(first_row, height):
    i0 = first_row + BR * jnp.arange(NB, dtype=jnp.int32)
    f0 = jnp.clip(i0 - R, 0, height - 45)
    start = jnp.clip(f0 - first_row + R, 0, ROWS - SR) // 8 * 8
    krow = lax.broadcasted_iota(jnp.int32, (ROWS, W, 128), 0) + (first_row - R)
    kcol = lax.broadcasted_iota(jnp.int32, (ROWS, W, 128), 1)
    lane = lax.broadcasted_iota(jnp.int32, (ROWS, W, 128), 2)
    f = jnp.clip(first_row + lane - R, 0, height - 45)
    row_out = (lane < T) & ((krow < f) | (krow >= f + 45))
    qcol = lane - T
    col_out = (lane >= T) & (lane < 2 * T) & ((kcol < qcol + 2) | (kcol > qcol + 46))
    aux = jnp.where(row_out | col_out, -1e30, 0.0).astype(BF).reshape(ROWS * W, 128)
    return start.astype(jnp.int32), aux


def spread(x, scale):
    x = (x.reshape(NB, 1, BR * T, 128) * scale).astype(BF)
    lane = lax.broadcasted_iota(jnp.int32, (1, 2, 1, 128), 3) // 64
    head = lax.broadcasted_iota(jnp.int32, (1, 2, 1, 128), 1)
    return jnp.where(lane == head, x, jnp.zeros((), BF)).reshape(NB, NQ, 128)


def with_marks(q):
    lane = lax.broadcasted_iota(jnp.int32, (NB, 2, BR, T, 128), 4)
    row = lax.broadcasted_iota(jnp.int32, (NB, 2, BR, T, 128), 0) * BR + lax.broadcasted_iota(jnp.int32, (NB, 2, BR, T, 128), 2)
    col = lax.broadcasted_iota(jnp.int32, (NB, 2, BR, T, 128), 3)
    mark = jnp.where((lane == row) | (lane == T + col), 1.0, 0.0).astype(BF).reshape(NB, NQ, 128)
    return jnp.concatenate([spread(q, 0.125), mark], axis=2)


def shift(x, axis, by, closed):
    n = lax.axis_size(axis)
    pairs = [(i, (i + by) % n) for i in range(n) if closed or 0 <= i + by < n]
    return lax.ppermute(x, axis, pairs)


def widen(x):
    return jnp.concatenate([shift(x, "lon", 1, True), x, shift(x, "lon", -1, True)], axis=1)


def heighten(mid):
    north = shift(mid[T - R :], "lat", 1, False)
    south = shift(mid[:R], "lat", -1, False)
    return jnp.concatenate([north, mid, south], axis=0).reshape(ROWS * W, 128)


def fold(north, mid, south):
    north = north.reshape(R, W, 128)
    south = south.reshape(R, W, 128)
    from_south = shift(north, "lat", -1, False).astype(F32)
    from_north = shift(south, "lat", 1, False).astype(F32)
    pad = ((T - R, 0), (0, 0), (0, 0)), ((0, T - R), (0, 0), (0, 0))
    mid = mid.reshape(T, W, 128) + jnp.pad(from_south, pad[0]) + jnp.pad(from_north, pad[1])
    from_east = shift(mid[:, :T].astype(BF), "lon", -1, True).astype(F32)
    from_west = shift(mid[:, 2 * T :].astype(BF), "lon", 1, True).astype(F32)
    return (mid[:, T : 2 * T] + from_east + from_west).astype(BF)


def body(queries, keys, values, out_grad):
    height = T * lax.axis_size("lat")
    k = widen(keys)
    v = widen(values)
    k, first_row, queries, out_grad = lax.optimization_barrier((k, lax.axis_index("lat") * T, queries, out_grad))
    k = heighten(k)
    v = heighten(v)
    start, aux = tables(first_row, height)
    q = with_marks(queries)
    g = spread(out_grad, 1.0)
    p, linv, gs, *dv = run_a(start, k, aux, q, g)
    grad_values = fold(*dv)
    attended, grad_queries, *dk = run_b(start, k, v, q, gs, p, linv)
    grad_keys = fold(*dk)
    return attended.reshape(T, T, 128), grad_queries.reshape(T, T, 128), grad_keys, grad_values


def solution(mesh):
    spec = P("lat", "lon", None)
    return jax.shard_map(body, mesh=mesh, in_specs=(spec,) * 4, out_specs=(spec,) * 4, check_vma=False)
```

```python
import jax
import jax.numpy as jnp
from jax import lax
from jax.experimental import pallas as pl
from jax.experimental.pallas import tpu as pltpu
from jax.sharding import PartitionSpec as P

R = 22
T = 24
W = 3 * T
ROWS = T + 2 * R
BR = 8
NB = T // BR
SR = BR + 2 * R
NK = SR * W
NQ = 2 * BR * T
CA = SR * W // 2
CB = SR * W
F32 = jnp.float32
BF = jnp.bfloat16
NT = (((1,), (1,)), ((), ()))
TN = (((0,), (0,)), ((), ()))


def kernel_a(start, k_ref, aux_ref, q_ref, g_ref, p_ref, linv_ref, gs_ref, vn_ref, vm_ref, vs_ref, s_scr, m_scr, acc):
    b = pl.program_id(0)
    here = lax.rem(b, 2)
    prior = jnp.maximum(b - 1, 0)
    base = pl.multiple_of(start[jnp.minimum(b, NB - 1)] * W, 64)
    prior_base = pl.multiple_of(start[prior] * W, 64)

    def rows(c, n=CA):
        return pl.ds(pl.multiple_of(c * n, 16), n)

    def scores(c, m, n=CA):
        at = pl.multiple_of(base + c * n, 16)
        lhs = jnp.concatenate([k_ref[pl.ds(at, n), :], aux_ref[pl.ds(at, n), :]], axis=1)
        s = lax.dot_general(lhs, q_ref[0], NT, preferred_element_type=F32)
        s_scr[here, rows(c, n), :] = s
        return jnp.maximum(m, jnp.max(s.reshape(n // 8, 8, NQ), axis=0))

    def expo(c, m, l, n=CA):
        p = jnp.exp(s_scr[1 - here, rows(c, n), :] - m)
        p_ref[0, rows(c, n), :] = p.astype(BF)
        return l + jnp.sum(p.reshape(n // 8, 8, NQ), axis=0)

    def close(m):
        m_scr[...] = jnp.broadcast_to(jnp.max(m, axis=0, keepdims=True), (8, NQ))

    c_parts = 13
    low = jnp.full((8, NQ), -3e38, F32)
    zero = jnp.zeros((8, NQ), F32)

    def finish(l):
        linv = 1.0 / jnp.sum(l, axis=0, keepdims=True)
        linv_ref[0] = jnp.broadcast_to(linv, (8, NQ))
        turned = jnp.transpose(jnp.broadcast_to(linv, (128, NQ)))
        gs_ref[0] = (g_ref[0].astype(F32) * turned).astype(BF)

    @pl.when(b == 0)
    def _():
        acc[...] = jnp.zeros_like(acc)
        close(lax.fori_loop(0, NK // CA, scores, low))

    @pl.when((b > 0) & (b < NB))
    def _():
        m = m_scr[:1]

        def both(c, carry):
            fresh, l = carry
            for part in range(c_parts):
                fresh = scores(c * c_parts + part, fresh, CA // c_parts)
                l = expo(c * c_parts + part, m, l, CA // c_parts)
            return fresh, l

        fresh, l = lax.fori_loop(0, NK // CA, both, (low, zero))
        close(fresh)
        finish(l)

    @pl.when(b == NB)
    def _():
        m = m_scr[:1]
        finish(lax.fori_loop(0, NK // CA, lambda c, l: expo(c, m, l), zero))

    @pl.when(b > 0)
    def _():
        gs = gs_ref[0]

        def dv(c, _):
            at = pl.multiple_of(prior_base + c * CA, 16)
            acc[pl.ds(at, CA), :] += jnp.dot(p_ref[0, rows(c), :], gs, preferred_element_type=F32)
            return 0

        lax.fori_loop(0, NK // CA, dv, 0)

    @pl.when(b == NB)
    def _():
        vn_ref[...] = acc[: R * W, :].astype(BF)
        vm_ref[...] = acc[R * W : (R + T) * W, :]
        vs_ref[...] = acc[(R + T) * W :, :].astype(BF)


def kernel_b(start, k_ref, v_ref, q_ref, gs_ref, p_ref, linv_ref, o_ref, dq_ref, kn_ref, km_ref, ks_ref, ot, acc):
    b = pl.program_id(0)
    base = pl.multiple_of(start[b] * W, 64)

    @pl.when(b == 0)
    def _():
        acc[...] = jnp.zeros_like(acc)

    q = q_ref[0][:, :128]
    gs = gs_ref[0]
    ot[...] = jnp.zeros_like(ot)

    def attend(c, _):
        at = pl.multiple_of(base + c * CB, 32)
        p = p_ref[0, pl.ds(pl.multiple_of(c * CB, 32), CB), :]
        ot[...] += lax.dot_general(v_ref[pl.ds(at, CB), :], p, TN, preferred_element_type=F32)
        return 0

    lax.fori_loop(0, NK // CB, attend, 0)
    lane = lax.broadcasted_iota(jnp.int32, (NQ // 2, 128), 1)
    o = jnp.transpose(ot[...] * linv_ref[0][:1])
    o_bf = o.astype(BF)
    o_ref[...] = jnp.where(lane < 64, o[: NQ // 2], o[NQ // 2 :]).astype(BF)
    row = jnp.sum(gs.astype(F32) * o_bf.astype(F32), axis=1, keepdims=True)
    corr = jnp.transpose(jnp.broadcast_to(row, (NQ, 128)))[:1]
    ot[...] = jnp.zeros_like(ot)

    def back(c, _):
        at = pl.multiple_of(base + c * CB, 32)
        p = p_ref[0, pl.ds(pl.multiple_of(c * CB, 32), CB), :]
        gw = lax.dot_general(v_ref[pl.ds(at, CB), :], gs, NT, preferred_element_type=F32)
        ds = (p.astype(F32) * (gw - corr)).astype(BF)
        acc[pl.ds(at, CB), :] += jnp.dot(ds, q, preferred_element_type=F32)
        ot[...] += lax.dot_general(k_ref[pl.ds(at, CB), :], ds, TN, preferred_element_type=F32)
        return 0

    lax.fori_loop(0, NK // CB, back, 0)
    dq = jnp.transpose(ot[...] * 0.125)
    dq_ref[...] = jnp.where(lane < 64, dq[: NQ // 2], dq[NQ // 2 :]).astype(BF)

    @pl.when(b == NB - 1)
    def _():
        kn_ref[...] = acc[: R * W, :].astype(BF)
        km_ref[...] = acc[R * W : (R + T) * W, :]
        ks_ref[...] = acc[(R + T) * W :, :].astype(BF)


def whole(shape):
    return pl.BlockSpec(shape, lambda b, s: (0,) * len(shape))


def per_block(shape):
    return pl.BlockSpec((1,) + shape, lambda b, s: (b,) + (0,) * len(shape))


def sds(shape, dtype):
    return jax.ShapeDtypeStruct(shape, dtype)


grads_shape = [sds((R * W, 128), BF), sds((T * W, 128), F32), sds((R * W, 128), BF)]
grads_spec = [whole((R * W, 128)), whole((T * W, 128)), whole((R * W, 128))]


def run_a(start, k, aux, q, g):
    def ahead(shape):
        return pl.BlockSpec((1,) + shape, lambda b, s: (jnp.minimum(b, NB - 1),) + (0,) * len(shape))

    def behind(shape):
        return pl.BlockSpec((1,) + shape, lambda b, s: (jnp.maximum(b - 1, 0),) + (0,) * len(shape))

    return pl.pallas_call(
        kernel_a,
        grid_spec=pltpu.PrefetchScalarGridSpec(
            num_scalar_prefetch=1,
            grid=(NB + 1,),
            in_specs=[whole((ROWS * W, 128)), whole((ROWS * W, 128)), ahead((NQ, 256)), behind((NQ, 128))],
            out_specs=[behind((NK, NQ)), behind((8, NQ)), behind((NQ, 128))] + grads_spec,
            scratch_shapes=[pltpu.VMEM((2, NK, NQ), F32), pltpu.VMEM((8, NQ), F32), pltpu.VMEM((ROWS * W, 128), F32)],
        ),
        out_shape=[sds((NB, NK, NQ), BF), sds((NB, 8, NQ), F32), sds((NB, NQ, 128), BF)] + grads_shape,
        compiler_params=pltpu.CompilerParams(vmem_limit_bytes=48 << 20),
        cost_estimate=pl.CostEstimate(flops=6_000_000_000, bytes_accessed=14_000_000, transcendentals=4_000_000),
        name="scores_and_dv",
    )(start, k, aux, q, g)


def run_b(start, k, v, q, gs, p, linv):
    return pl.pallas_call(
        kernel_b,
        grid_spec=pltpu.PrefetchScalarGridSpec(
            num_scalar_prefetch=1,
            grid=(NB,),
            in_specs=[whole((ROWS * W, 128)), whole((ROWS * W, 128)), per_block((NQ, 256)), per_block((NQ, 128)), per_block((NK, NQ)), per_block((8, NQ))],
            out_specs=[pl.BlockSpec((NQ // 2, 128), lambda b, s: (b, 0)), pl.BlockSpec((NQ // 2, 128), lambda b, s: (b, 0))] + grads_spec,
            scratch_shapes=[pltpu.VMEM((128, NQ), F32), pltpu.VMEM((ROWS * W, 128), F32)],
        ),
        out_shape=[sds((T * T, 128), BF), sds((T * T, 128), BF)] + grads_shape,
        compiler_params=pltpu.CompilerParams(vmem_limit_bytes=48 << 20),
        cost_estimate=pl.CostEstimate(flops=8_000_000_000, bytes_accessed=14_000_000, transcendentals=0),
        name="attended_and_dk",
    )(start, k, v, q, gs, p, linv)


def tables(first_row, height):
    i0 = first_row + BR * jnp.arange(NB, dtype=jnp.int32)
    f0 = jnp.clip(i0 - R, 0, height - 45)
    start = jnp.clip(f0 - first_row + R, 0, ROWS - SR) // 8 * 8
    krow = lax.broadcasted_iota(jnp.int32, (ROWS, W, 128), 0) + (first_row - R)
    kcol = lax.broadcasted_iota(jnp.int32, (ROWS, W, 128), 1)
    lane = lax.broadcasted_iota(jnp.int32, (ROWS, W, 128), 2)
    f = jnp.clip(first_row + lane - R, 0, height - 45)
    row_out = (lane < T) & ((krow < f) | (krow >= f + 45))
    qcol = lane - T
    col_out = (lane >= T) & (lane < 2 * T) & ((kcol < qcol + 2) | (kcol > qcol + 46))
    aux = jnp.where(row_out | col_out, -1e30, 0.0).astype(BF).reshape(ROWS * W, 128)
    return start.astype(jnp.int32), aux


def spread(x, scale):
    x = (x.reshape(NB, 1, BR * T, 128) * scale).astype(BF)
    lane = lax.broadcasted_iota(jnp.int32, (1, 2, 1, 128), 3) // 64
    head = lax.broadcasted_iota(jnp.int32, (1, 2, 1, 128), 1)
    return jnp.where(lane == head, x, jnp.zeros((), BF)).reshape(NB, NQ, 128)


def with_marks(q):
    lane = lax.broadcasted_iota(jnp.int32, (NB, 2, BR, T, 128), 4)
    row = lax.broadcasted_iota(jnp.int32, (NB, 2, BR, T, 128), 0) * BR + lax.broadcasted_iota(jnp.int32, (NB, 2, BR, T, 128), 2)
    col = lax.broadcasted_iota(jnp.int32, (NB, 2, BR, T, 128), 3)
    mark = jnp.where((lane == row) | (lane == T + col), 1.0, 0.0).astype(BF).reshape(NB, NQ, 128)
    return jnp.concatenate([spread(q, 0.125), mark], axis=2)


def shift(x, axis, by, closed):
    n = lax.axis_size(axis)
    pairs = [(i, (i + by) % n) for i in range(n) if closed or 0 <= i + by < n]
    return lax.ppermute(x, axis, pairs)


def widen(x):
    return jnp.concatenate([shift(x, "lon", 1, True), x, shift(x, "lon", -1, True)], axis=1)


def heighten(mid):
    north = shift(mid[T - R :], "lat", 1, False)
    south = shift(mid[:R], "lat", -1, False)
    return jnp.concatenate([north, mid, south], axis=0).reshape(ROWS * W, 128)


def fold(north, mid, south):
    north = north.reshape(R, W, 128)
    south = south.reshape(R, W, 128)
    from_south = shift(north, "lat", -1, False).astype(F32)
    from_north = shift(south, "lat", 1, False).astype(F32)
    pad = ((T - R, 0), (0, 0), (0, 0)), ((0, T - R), (0, 0), (0, 0))
    mid = mid.reshape(T, W, 128) + jnp.pad(from_south, pad[0]) + jnp.pad(from_north, pad[1])
    from_east = shift(mid[:, :T].astype(BF), "lon", -1, True).astype(F32)
    from_west = shift(mid[:, 2 * T :].astype(BF), "lon", 1, True).astype(F32)
    return (mid[:, T : 2 * T] + from_east + from_west).astype(BF)


def body(queries, keys, values, out_grad):
    height = T * lax.axis_size("lat")
    k = widen(keys)
    k, values, first_row, queries, out_grad = lax.optimization_barrier(
        (k, values, lax.axis_index("lat") * T, queries, out_grad)
    )
    k = heighten(k)
    v = widen(values)
    v = heighten(v)
    start, aux = tables(first_row, height)
    q = with_marks(queries)
    g = spread(out_grad, 1.0)
    p, linv, gs, *dv = run_a(start, k, aux, q, g)
    grad_values = fold(*dv)
    attended, grad_queries, *dk = run_b(start, k, v, q, gs, p, linv)
    grad_keys = fold(*dk)
    return attended.reshape(T, T, 128), grad_queries.reshape(T, T, 128), grad_keys, grad_values


def solution(mesh):
    spec = P("lat", "lon", None)
    return jax.shard_map(body, mesh=mesh, in_specs=(spec,) * 4, out_specs=(spec,) * 4, check_vma=False)
```

```python
import jax
import jax.numpy as jnp
from jax import lax
from jax.experimental import pallas as pl
from jax.experimental.pallas import tpu as pltpu
from jax.sharding import PartitionSpec as P


R = 22
T = 24
W = 3 * T
ROWS = T + 2 * R
BR = 8
NB = T // BR
SR = BR + 2 * R
NK = SR * W
NQ = 2 * BR * T
CA = SR * W // 2
CB = SR * W
F32 = jnp.float32
BF = jnp.bfloat16
NT = (((1,), (1,)), ((), ()))
TN = (((0,), (0,)), ((), ()))


def kernel_a(start, k_ref, aux_ref, q_ref, g_ref, p_ref, linv_ref, gs_ref, vn_ref, vm_ref, vs_ref, s_scr, m_scr, acc):
    b = pl.program_id(0)
    here = lax.rem(b, 2)
    prior = jnp.maximum(b - 1, 0)
    base = pl.multiple_of(start[jnp.minimum(b, NB - 1)] * W, 64)
    prior_base = pl.multiple_of(start[prior] * W, 64)

    def rows(c, n=CA):
        return pl.ds(pl.multiple_of(c * n, 16), n)

    def scores(c, m, n=CA):
        at = pl.multiple_of(base + c * n, 16)
        lhs = jnp.concatenate([k_ref[pl.ds(at, n), :], aux_ref[pl.ds(at, n), :]], axis=1)
        s = lax.dot_general(lhs, q_ref[0], NT, preferred_element_type=F32)
        s_scr[here, rows(c, n), :] = s
        return jnp.maximum(m, jnp.max(s.reshape(n // 8, 8, NQ), axis=0))

    def expo(c, m, l, n=CA):
        p = jnp.exp(s_scr[1 - here, rows(c, n), :] - m)
        p_ref[0, rows(c, n), :] = p.astype(BF)
        return l + jnp.sum(p.reshape(n // 8, 8, NQ), axis=0)

    def close(m):
        m_scr[...] = jnp.broadcast_to(jnp.max(m, axis=0, keepdims=True), (8, NQ))

    c_parts = 13
    low = jnp.full((8, NQ), -3e38, F32)
    zero = jnp.zeros((8, NQ), F32)

    def finish(l):
        linv = 1.0 / jnp.sum(l, axis=0, keepdims=True)
        linv_ref[0] = jnp.broadcast_to(linv, (8, NQ))
        turned = jnp.transpose(jnp.broadcast_to(linv, (128, NQ)))
        gs_ref[0] = (g_ref[0].astype(F32) * turned).astype(BF)

    @pl.when(b == 0)
    def _():
        acc[...] = jnp.zeros_like(acc)
        close(lax.fori_loop(0, NK // CA, scores, low))

    @pl.when((b > 0) & (b < NB))
    def _():
        m = m_scr[:1]

        def both(c, carry):
            fresh, l = carry
            for part in range(c_parts):
                fresh = scores(c * c_parts + part, fresh, CA // c_parts)
                l = expo(c * c_parts + part, m, l, CA // c_parts)
            return fresh, l

        fresh, l = lax.fori_loop(0, NK // CA, both, (low, zero))
        close(fresh)
        finish(l)

    @pl.when(b == NB)
    def _():
        m = m_scr[:1]
        finish(lax.fori_loop(0, NK // CA, lambda c, l: expo(c, m, l), zero))

    @pl.when(b > 0)
    def _():
        gs = gs_ref[0]

        def dv(c, _):
            at = pl.multiple_of(prior_base + c * CA, 16)
            acc[pl.ds(at, CA), :] += jnp.dot(p_ref[0, rows(c), :], gs, preferred_element_type=F32)
            return 0

        lax.fori_loop(0, NK // CA, dv, 0)

    @pl.when(b == NB)
    def _():
        vn_ref[...] = acc[: R * W, :].astype(BF)
        vm_ref[...] = acc[R * W : (R + T) * W, :]
        vs_ref[...] = acc[(R + T) * W :, :].astype(BF)


def kernel_b(start, k_ref, v_ref, q_ref, gs_ref, p_ref, linv_ref, o_ref, dq_ref, kn_ref, km_ref, ks_ref, ot, acc):
    b = pl.program_id(0)
    base = pl.multiple_of(start[b] * W, 64)

    @pl.when(b == 0)
    def _():
        acc[...] = jnp.zeros_like(acc)

    q = q_ref[0][:, :128]
    gs = gs_ref[0]
    ot[...] = jnp.zeros_like(ot)

    def attend(c, _):
        at = pl.multiple_of(base + c * CB, 32)
        p = p_ref[0, pl.ds(pl.multiple_of(c * CB, 32), CB), :]
        ot[...] += lax.dot_general(v_ref[pl.ds(at, CB), :], p, TN, preferred_element_type=F32)
        return 0

    lax.fori_loop(0, NK // CB, attend, 0)
    lane = lax.broadcasted_iota(jnp.int32, (NQ // 2, 128), 1)
    o = jnp.transpose(ot[...] * linv_ref[0][:1])
    o_bf = o.astype(BF)
    o_ref[...] = jnp.where(lane < 64, o[: NQ // 2], o[NQ // 2 :]).astype(BF)
    row = jnp.sum(gs.astype(F32) * o_bf.astype(F32), axis=1, keepdims=True)
    corr = jnp.transpose(jnp.broadcast_to(row, (NQ, 128)))[:1]
    ot[...] = jnp.zeros_like(ot)

    def back(c, _):
        at = pl.multiple_of(base + c * CB, 32)
        p = p_ref[0, pl.ds(pl.multiple_of(c * CB, 32), CB), :]
        gw = lax.dot_general(v_ref[pl.ds(at, CB), :], gs, NT, preferred_element_type=F32)
        ds = (p.astype(F32) * (gw - corr)).astype(BF)
        acc[pl.ds(at, CB), :] += jnp.dot(ds, q, preferred_element_type=F32)
        ot[...] += lax.dot_general(k_ref[pl.ds(at, CB), :], ds, TN, preferred_element_type=F32)
        return 0

    lax.fori_loop(0, NK // CB, back, 0)
    dq = jnp.transpose(ot[...] * 0.125)
    dq_ref[...] = jnp.where(lane < 64, dq[: NQ // 2], dq[NQ // 2 :]).astype(BF)

    @pl.when(b == NB - 1)
    def _():
        kn_ref[...] = acc[: R * W, :].astype(BF)
        km_ref[...] = acc[R * W : (R + T) * W, :]
        ks_ref[...] = acc[(R + T) * W :, :].astype(BF)


def whole(shape):
    return pl.BlockSpec(shape, lambda b, s: (0,) * len(shape))


def per_block(shape):
    return pl.BlockSpec((1,) + shape, lambda b, s: (b,) + (0,) * len(shape))


def sds(shape, dtype):
    return jax.ShapeDtypeStruct(shape, dtype)


grads_shape = [sds((R * W, 128), BF), sds((T * W, 128), F32), sds((R * W, 128), BF)]
grads_spec = [whole((R * W, 128)), whole((T * W, 128)), whole((R * W, 128))]


def run_a(start, k, aux, q, g):
    def ahead(shape):
        return pl.BlockSpec((1,) + shape, lambda b, s: (jnp.minimum(b, NB - 1),) + (0,) * len(shape))

    def behind(shape):
        return pl.BlockSpec((1,) + shape, lambda b, s: (jnp.maximum(b - 1, 0),) + (0,) * len(shape))

    return pl.pallas_call(
        kernel_a,
        grid_spec=pltpu.PrefetchScalarGridSpec(
            num_scalar_prefetch=1,
            grid=(NB + 1,),
            in_specs=[whole((ROWS * W, 128)), whole((ROWS * W, 128)), ahead((NQ, 256)), behind((NQ, 128))],
            out_specs=[behind((NK, NQ)), behind((8, NQ)), behind((NQ, 128))] + grads_spec,
            scratch_shapes=[pltpu.VMEM((2, NK, NQ), F32), pltpu.VMEM((8, NQ), F32), pltpu.VMEM((ROWS * W, 128), F32)],
        ),
        out_shape=[sds((NB, NK, NQ), BF), sds((NB, 8, NQ), F32), sds((NB, NQ, 128), BF)] + grads_shape,
        compiler_params=pltpu.CompilerParams(vmem_limit_bytes=48 << 20),
        cost_estimate=pl.CostEstimate(flops=6_000_000_000, bytes_accessed=14_000_000, transcendentals=4_000_000),
        name="scores_and_dv",
    )(start, k, aux, q, g)


def run_b(start, k, v, q, gs, p, linv):
    return pl.pallas_call(
        kernel_b,
        grid_spec=pltpu.PrefetchScalarGridSpec(
            num_scalar_prefetch=1,
            grid=(NB,),
            in_specs=[whole((ROWS * W, 128)), whole((ROWS * W, 128)), per_block((NQ, 256)), per_block((NQ, 128)), per_block((NK, NQ)), per_block((8, NQ))],
            out_specs=[pl.BlockSpec((NQ // 2, 128), lambda b, s: (b, 0)), pl.BlockSpec((NQ // 2, 128), lambda b, s: (b, 0))] + grads_spec,
            scratch_shapes=[pltpu.VMEM((128, NQ), F32), pltpu.VMEM((ROWS * W, 128), F32)],
        ),
        out_shape=[sds((T * T, 128), BF), sds((T * T, 128), BF)] + grads_shape,
        compiler_params=pltpu.CompilerParams(vmem_limit_bytes=48 << 20),
        cost_estimate=pl.CostEstimate(flops=8_000_000_000, bytes_accessed=14_000_000, transcendentals=0),
        name="attended_and_dk",
    )(start, k, v, q, gs, p, linv)


def tables(first_row, height):
    i0 = first_row + BR * jnp.arange(NB, dtype=jnp.int32)
    f0 = jnp.clip(i0 - R, 0, height - 45)
    start = jnp.clip(f0 - first_row + R, 0, ROWS - SR) // 8 * 8
    krow = lax.broadcasted_iota(jnp.int32, (ROWS, W, 128), 0) + (first_row - R)
    kcol = lax.broadcasted_iota(jnp.int32, (ROWS, W, 128), 1)
    lane = lax.broadcasted_iota(jnp.int32, (ROWS, W, 128), 2)
    f = jnp.clip(first_row + lane - R, 0, height - 45)
    row_out = (lane < T) & ((krow < f) | (krow >= f + 45))
    qcol = lane - T
    col_out = (lane >= T) & (lane < 2 * T) & ((kcol < qcol + 2) | (kcol > qcol + 46))
    aux = jnp.where(row_out | col_out, -1e30, 0.0).astype(BF).reshape(ROWS * W, 128)
    return start.astype(jnp.int32), aux


def spread(x, scale):
    x = (x.reshape(NB, 1, BR * T, 128) * scale).astype(BF)
    lane = lax.broadcasted_iota(jnp.int32, (1, 2, 1, 128), 3) // 64
    head = lax.broadcasted_iota(jnp.int32, (1, 2, 1, 128), 1)
    return jnp.where(lane == head, x, jnp.zeros((), BF)).reshape(NB, NQ, 128)


def with_marks(q):
    lane = lax.broadcasted_iota(jnp.int32, (NB, 2, BR, T, 128), 4)
    row = lax.broadcasted_iota(jnp.int32, (NB, 2, BR, T, 128), 0) * BR + lax.broadcasted_iota(jnp.int32, (NB, 2, BR, T, 128), 2)
    col = lax.broadcasted_iota(jnp.int32, (NB, 2, BR, T, 128), 3)
    mark = jnp.where((lane == row) | (lane == T + col), 1.0, 0.0).astype(BF).reshape(NB, NQ, 128)
    return jnp.concatenate([spread(q, 0.125), mark], axis=2)


def shift(x, by):
    n = lax.axis_size("lat")
    return lax.ppermute(x, "lat", [(i, i + by) for i in range(n) if 0 <= i + by < n])


def swap(x, first):
    n = lax.axis_size("lon")
    pairs = [(i % n, (i + 1) % n) for i in range(first, n + first, 2)]
    return lax.ppermute(x, "lon", pairs + [(b, a) for a, b in pairs])


def heighten(mid):
    north = shift(mid[T - R :], 1)
    south = shift(mid[:R], -1)
    return jnp.concatenate([north, mid, south], axis=0).reshape(ROWS * W, 128)


def fold_lat(north, mid, south):
    from_south = shift(north.reshape(R, W, 128), -1).astype(F32)
    from_north = shift(south.reshape(R, W, 128), 1).astype(F32)
    pad = ((T - R, 0), (0, 0), (0, 0)), ((0, T - R), (0, 0), (0, 0))
    return mid.reshape(T, W, 128) + jnp.pad(from_south, pad[0]) + jnp.pad(from_north, pad[1])


def body(queries, keys, values, out_grad):
    height = T * lax.axis_size("lat")
    even = lax.axis_index("lon") % 2 == 0
    pair = jnp.stack([keys, values])
    near, far = swap(pair, 0), swap(pair, 1)

    def widen(x, i):
        return jnp.concatenate([jnp.where(even, far[i], near[i]), x, jnp.where(even, near[i], far[i])], axis=1)

    k = widen(keys, 0)
    v = widen(values, 1)
    k, first_row, queries, out_grad = lax.optimization_barrier((k, lax.axis_index("lat") * T, queries, out_grad))
    k = heighten(k)
    v = heighten(v)
    start, aux = tables(first_row, height)
    q = with_marks(queries)
    g = spread(out_grad, 1.0)
    p, linv, gs, *dv = run_a(start, k, aux, q, g)
    dv = fold_lat(*dv)
    attended, grad_queries, *dk = run_b(start, k, v, q, gs, p, linv)
    dk = fold_lat(*dk)
    west = [x[:, :T].astype(BF) for x in (dk, dv)]
    east = [x[:, 2 * T :].astype(BF) for x in (dk, dv)]
    near = swap(jnp.stack([jnp.where(even, e, w) for e, w in zip(east, west)]), 0)
    far = swap(jnp.stack([jnp.where(even, w, e) for e, w in zip(east, west)]), 1)
    grads = [(x[:, T : 2 * T] + near[i].astype(F32) + far[i].astype(F32)).astype(BF) for i, x in enumerate((dk, dv))]
    return attended.reshape(T, T, 128), grad_queries.reshape(T, T, 128), grads[0], grads[1]


def solution(mesh):
    spec = P("lat", "lon", None)
    return jax.shard_map(body, mesh=mesh, in_specs=(spec,) * 4, out_specs=(spec,) * 4, check_vma=False)
```

```python
import jax
import jax.numpy as jnp
from jax import lax
from jax.experimental import pallas as pl
from jax.experimental.pallas import tpu as pltpu
from jax.sharding import PartitionSpec as P


R = 22
T = 24
W = 3 * T
BR = 8
NB = T // BR
SR = BR + 2 * R
NQ = 2 * BR * T
MID = T * W
EDGE = R * W
FAR = (SR - T) * W
NK = MID + FAR
PART = 2 * W
F32 = jnp.float32
BF = jnp.bfloat16
NT = (((1,), (1,)), ((), ()))
TN = (((0,), (0,)), ((), ()))


def far_base(start, b):
    return pl.multiple_of(start[b] * W, 64)


def kernel_a(start, km_ref, kf_ref, am_ref, af_ref, q_ref, g_ref, pm_ref, pf_ref, linv_ref, gs_ref, vf_ref, s_scr, m_scr, acc):
    b = pl.program_id(0)
    here = lax.rem(b, 2)
    base = far_base(start, jnp.minimum(b, NB - 1))
    prior_base = far_base(start, jnp.maximum(b - 1, 0))

    def scores(part, at, n, m):
        at = pl.multiple_of(at, 16)
        if part == 0:
            rows = pl.ds(at, n)
            lhs = jnp.concatenate([km_ref[rows, :], am_ref[rows, :]], axis=1)
        else:
            rows = pl.ds(pl.multiple_of(base + at, 16), n)
            lhs = jnp.concatenate([kf_ref[rows, :], af_ref[rows, :]], axis=1)
        s = lax.dot_general(lhs, q_ref[0], NT, preferred_element_type=F32)
        s_scr[here, pl.ds(at + part * MID, n), :] = s
        return jnp.maximum(m, jnp.max(s.reshape(n // 8, 8, NQ), axis=0))

    def expo(part, at, n, m, l):
        at = pl.multiple_of(at, 16)
        p = jnp.exp(s_scr[1 - here, pl.ds(at + part * MID, n), :] - m)
        (pm_ref, pf_ref)[part][0, pl.ds(at, n), :] = p.astype(BF)
        return l + jnp.sum(p.reshape(n // 8, 8, NQ), axis=0)

    def close(m):
        m_scr[...] = jnp.broadcast_to(jnp.max(m, axis=0, keepdims=True), (8, NQ))

    def finish(l):
        linv = 1.0 / jnp.sum(l, axis=0, keepdims=True)
        linv_ref[0] = jnp.broadcast_to(linv, (8, NQ))
        turned = jnp.transpose(jnp.broadcast_to(linv, (128, NQ)))
        gs_ref[0] = (g_ref[0].astype(F32) * turned).astype(BF)

    low = jnp.full((8, NQ), -3e38, F32)
    zero = jnp.zeros((8, NQ), F32)

    @pl.when(b == 0)
    def _():
        acc[...] = jnp.zeros_like(acc)
        close(scores(1, 0, FAR, scores(0, 0, MID, low)))

    @pl.when((b > 0) & (b < NB))
    def _():
        m = m_scr[:1]
        carry = low, zero
        for part, many, parts in ((0, MID // PART, 6), (1, FAR // PART, 7)):

            def both(c, carry, part=part, parts=parts):
                fresh, l = carry
                for i in range(parts):
                    fresh = scores(part, (c * parts + i) * PART, PART, fresh)
                    l = expo(part, (c * parts + i) * PART, PART, m, l)
                return fresh, l

            carry = lax.fori_loop(0, many // parts, both, carry)
        close(carry[0])
        finish(carry[1])

    @pl.when(b == NB)
    def _():
        m, l = m_scr[:1], zero
        for part, n in ((0, MID // 2), (1, FAR // 2)):
            l = lax.fori_loop(0, 2, lambda c, l, part=part, n=n: expo(part, c * n, n, m, l), l)
        finish(l)

    @pl.when(b > 0)
    def _():
        acc[pl.ds(prior_base, FAR), :] += jnp.dot(pf_ref[0], gs_ref[0], preferred_element_type=F32)

    @pl.when(b == NB)
    def _():
        vf_ref[...] = acc[...].astype(BF)


def score_grads(p, v, gs, corr):
    gw = lax.dot_general(v, gs, NT, preferred_element_type=F32)
    return (p.astype(F32) * (gw - corr)).astype(BF)


def kernel_far(start, kf_ref, vm_ref, vf_ref, q_ref, gs_ref, pm_ref, pf_ref, linv_ref, dvf_ref, o_ref, corr_ref, dqt_ref, north_ref, south_ref, acc):
    b = pl.program_id(0)
    rows = pl.ds(far_base(start, b), FAR)

    @pl.when(b == 0)
    def _():
        acc[...] = jnp.zeros_like(acc)
        north_ref[1] = dvf_ref[:EDGE, :]
        south_ref[1] = dvf_ref[EDGE:, :]

    gs = gs_ref[0]
    ot = lax.dot_general(vm_ref[...], pm_ref[0], TN, preferred_element_type=F32)
    ot += lax.dot_general(vf_ref[rows, :], pf_ref[0], TN, preferred_element_type=F32)
    lane = lax.broadcasted_iota(jnp.int32, (NQ // 2, 128), 1)
    o = jnp.transpose(ot * linv_ref[0][:1])
    o_ref[...] = jnp.where(lane < 64, o[: NQ // 2], o[NQ // 2 :]).astype(BF)
    row = jnp.sum(gs.astype(F32) * o.astype(BF).astype(F32), axis=1, keepdims=True)
    corr = jnp.transpose(jnp.broadcast_to(row, (NQ, 128)))
    corr_ref[0] = corr[:8]
    ds = score_grads(pf_ref[0], vf_ref[rows, :], gs, corr[:1])
    acc[rows, :] += jnp.dot(ds, q_ref[0][:, :128], preferred_element_type=F32)
    dqt_ref[0] = lax.dot_general(kf_ref[rows, :], ds, TN, preferred_element_type=F32)

    @pl.when(b == NB - 1)
    def _():
        north_ref[0] = acc[:EDGE, :].astype(BF)
        south_ref[0] = acc[EDGE:, :].astype(BF)


def kernel_mid(start, km_ref, vm_ref, q_ref, gs_ref, pm_ref, corr_ref, dqt_ref, dq_ref, grads_ref):
    b = pl.program_id(0)

    @pl.when(b == 0)
    def _():
        grads_ref[...] = jnp.zeros_like(grads_ref)

    gs = gs_ref[0]
    ds = score_grads(pm_ref[0], vm_ref[...], gs, corr_ref[0][:1])
    grads_ref[0] += jnp.dot(ds, q_ref[0][:, :128], preferred_element_type=F32)
    dqt = dqt_ref[0] + lax.dot_general(km_ref[...], ds, TN, preferred_element_type=F32)
    grads_ref[1] += jnp.dot(pm_ref[0], gs, preferred_element_type=F32)
    lane = lax.broadcasted_iota(jnp.int32, (NQ // 2, 128), 1)
    dq = jnp.transpose(dqt * 0.125)
    dq_ref[...] = jnp.where(lane < 64, dq[: NQ // 2], dq[NQ // 2 :]).astype(BF)


def whole(*shape):
    return pl.BlockSpec(shape, lambda b, s: (0,) * len(shape))


def per_block(*shape, at=lambda b: b):
    return pl.BlockSpec((1,) + shape, lambda b, s: (at(b),) + (0,) * len(shape))


def rows_of_block():
    return pl.BlockSpec((NQ // 2, 128), lambda b, s: (b, 0))


def sds(*shape, dtype=BF):
    return jax.ShapeDtypeStruct(shape, dtype)


def call(kernel, grid, in_specs, out_specs, out_shape, scratch, flops):
    return pl.pallas_call(
        kernel,
        grid_spec=pltpu.PrefetchScalarGridSpec(
            num_scalar_prefetch=1, grid=(grid,), in_specs=in_specs, out_specs=out_specs, scratch_shapes=scratch
        ),
        out_shape=out_shape,
        compiler_params=pltpu.CompilerParams(vmem_limit_bytes=48 << 20),
        cost_estimate=pl.CostEstimate(flops=flops, bytes_accessed=14_000_000, transcendentals=0),
    )


def run_a(start, km, kf, am, af, q, g):
    ahead = lambda b: jnp.minimum(b, NB - 1)
    behind = lambda b: jnp.maximum(b - 1, 0)
    return call(
        kernel_a,
        NB + 1,
        [whole(MID, 128), whole(2 * EDGE, 128)] * 2 + [per_block(NQ, 256, at=ahead), per_block(NQ, 128, at=behind)],
        [per_block(*x, at=behind) for x in ((MID, NQ), (FAR, NQ), (8, NQ), (NQ, 128))] + [whole(2 * EDGE, 128)],
        [sds(NB, MID, NQ), sds(NB, FAR, NQ), sds(NB, 8, NQ, dtype=F32), sds(NB, NQ, 128), sds(2 * EDGE, 128)],
        [pltpu.VMEM((2, NK, NQ), F32), pltpu.VMEM((8, NQ), F32), pltpu.VMEM((2 * EDGE, 128), F32)],
        5_000_000_000,
    )(start, km, kf, am, af, q, g)


def run_far(start, kf, vm, vf, q, gs, pm, pf, linv, dvf):
    return call(
        kernel_far,
        NB,
        [whole(2 * EDGE, 128), whole(MID, 128), whole(2 * EDGE, 128), per_block(NQ, 256), per_block(NQ, 128)]
        + [per_block(MID, NQ), per_block(FAR, NQ), per_block(8, NQ), whole(2 * EDGE, 128)],
        [rows_of_block(), per_block(8, NQ), per_block(128, NQ), whole(2, EDGE, 128), whole(2, EDGE, 128)],
        [sds(T * T, 128), sds(NB, 8, NQ, dtype=F32), sds(NB, 128, NQ, dtype=F32), sds(2, EDGE, 128), sds(2, EDGE, 128)],
        [pltpu.VMEM((2 * EDGE, 128), F32)],
        5_000_000_000,
    )(start, kf, vm, vf, q, gs, pm, pf, linv, dvf)


def run_mid(start, km, vm, q, gs, pm, corr, dqt):
    return call(
        kernel_mid,
        NB,
        [whole(MID, 128), whole(MID, 128), per_block(NQ, 256), per_block(NQ, 128), per_block(MID, NQ)]
        + [per_block(8, NQ), per_block(128, NQ)],
        [rows_of_block(), whole(2, MID, 128)],
        [sds(T * T, 128), sds(2, MID, 128, dtype=F32)],
        [],
        5_000_000_000,
    )(start, km, vm, q, gs, pm, corr, dqt)


def tables(first_row, height):
    i0 = first_row + BR * jnp.arange(NB, dtype=jnp.int32)
    f0 = jnp.clip(i0 - R, 0, height - 45)
    start = jnp.clip(f0 - first_row + R, 0, T - BR) // 8 * 8

    def lanes(krow, n):
        krow = krow + (first_row - R)
        kcol = lax.broadcasted_iota(jnp.int32, (n, W, 128), 1)
        lane = lax.broadcasted_iota(jnp.int32, (n, W, 128), 2)
        f = jnp.clip(first_row + lane - R, 0, height - 45)
        row_out = (lane < T) & ((krow < f) | (krow >= f + 45))
        qcol = lane - T
        col_out = (lane >= T) & (lane < 2 * T) & ((kcol < qcol + 2) | (kcol > qcol + 46))
        return jnp.where(row_out | col_out, -1e30, 0.0).astype(BF).reshape(n * W, 128)

    far = lax.broadcasted_iota(jnp.int32, (2 * R, W, 128), 0)
    mid = lax.broadcasted_iota(jnp.int32, (T, W, 128), 0) + R
    return start.astype(jnp.int32), lanes(mid, T), lanes(far + jnp.where(far >= R, T, 0), 2 * R)


def spread(x, scale):
    x = (x.reshape(NB, 1, BR * T, 128) * scale).astype(BF)
    lane = lax.broadcasted_iota(jnp.int32, (1, 2, 1, 128), 3) // 64
    head = lax.broadcasted_iota(jnp.int32, (1, 2, 1, 128), 1)
    return jnp.where(lane == head, x, jnp.zeros((), BF)).reshape(NB, NQ, 128)


def with_marks(q):
    lane = lax.broadcasted_iota(jnp.int32, (NB, 2, BR, T, 128), 4)
    row = lax.broadcasted_iota(jnp.int32, (NB, 2, BR, T, 128), 0) * BR + lax.broadcasted_iota(jnp.int32, (NB, 2, BR, T, 128), 2)
    col = lax.broadcasted_iota(jnp.int32, (NB, 2, BR, T, 128), 3)
    mark = jnp.where((lane == row) | (lane == T + col), 1.0, 0.0).astype(BF).reshape(NB, NQ, 128)
    return jnp.concatenate([spread(q, 0.125), mark], axis=2)


def shift(x, by):
    n = lax.axis_size("lat")
    return lax.ppermute(x, "lat", [(i, i + by) for i in range(n) if 0 <= i + by < n])


def swap(x, first):
    n = lax.axis_size("lon")
    pairs = [(i % n, (i + 1) % n) for i in range(first, n + first, 2)]
    return lax.ppermute(x, "lon", pairs + [(b, a) for a, b in pairs])


def far_rows(mid):
    return jnp.concatenate([shift(mid[T - R :], 1), shift(mid[:R], -1)], axis=0).reshape(2 * EDGE, 128)


def body(queries, keys, values, out_grad):
    height = T * lax.axis_size("lat")
    even = lax.axis_index("lon") % 2 == 0
    start, am, af = tables(lax.axis_index("lat") * T, height)
    q = with_marks(queries)
    g = spread(out_grad, 1.0)
    pair = jnp.stack([keys, values])
    near, far = swap(pair, 0), swap(pair, 1)

    def widen(x, i):
        return jnp.concatenate([jnp.where(even, far[i], near[i]), x, jnp.where(even, near[i], far[i])], axis=1)

    km = widen(keys, 0)
    vm = widen(values, 1)
    kf = far_rows(km)
    vf = far_rows(vm)
    km = km.reshape(MID, 128)
    vm = vm.reshape(MID, 128)
    pm, pf, linv, gs, dvf = run_a(start, km, kf, am, af, q, g)
    attended, corr, dqt, north, south = run_far(start, kf, vm, vf, q, gs, pm, pf, linv, dvf)
    from_south = shift(north, -1).reshape(2, R, W, 128)
    from_north = shift(south, 1).reshape(2, R, W, 128)
    grad_queries, mid = run_mid(start, km, vm, q, gs, pm, corr, dqt)
    none = (0, 0)
    mid = mid.reshape(2, T, W, 128)
    mid = mid + jnp.pad(from_south.astype(F32), (none, (T - R, 0), none, none))
    mid = mid + jnp.pad(from_north.astype(F32), (none, (0, T - R), none, none))
    west = mid[:, :, :T].astype(BF)
    east = mid[:, :, 2 * T :].astype(BF)
    near = swap(jnp.where(even, east, west), 0)
    far = swap(jnp.where(even, west, east), 1)
    grads = [(mid[i, :, T : 2 * T] + near[i].astype(F32) + far[i].astype(F32)).astype(BF) for i in range(2)]
    return attended.reshape(T, T, 128), grad_queries.reshape(T, T, 128), grads[0], grads[1]


def solution(mesh):
    spec = P("lat", "lon", None)
    return jax.shard_map(body, mesh=mesh, in_specs=(spec,) * 4, out_specs=(spec,) * 4, check_vma=False)
```

```python
import jax
import jax.numpy as jnp
from jax import lax
from jax.experimental import pallas as pl
from jax.experimental.pallas import tpu as pltpu
from jax.sharding import PartitionSpec as P


R = 22
T = 24
W = 3 * T
BR = 8
NB = T // BR
SR = BR + 2 * R
NQ = 2 * BR * T
MID = T * W
EDGE = R * W
FAR = (SR - T) * W
NK = MID + FAR
PART = 2 * W
F32 = jnp.float32
BF = jnp.bfloat16
NT = (((1,), (1,)), ((), ()))
TN = (((0,), (0,)), ((), ()))


def far_base(start, b):
    return pl.multiple_of(start[b] * W, 64)


def kernel_a(start, km_ref, kf_ref, am_ref, af_ref, q_ref, g_ref, pm_ref, pf_ref, linv_ref, gs_ref, north_ref, south_ref, s_scr, m_scr, acc):
    b = pl.program_id(0)
    here = lax.rem(b, 2)
    base = far_base(start, jnp.minimum(b, NB - 1))
    prior_base = far_base(start, jnp.maximum(b - 1, 0))

    def scores(part, at, n, m):
        at = pl.multiple_of(at, 16)
        if part == 0:
            rows = pl.ds(at, n)
            lhs = jnp.concatenate([km_ref[rows, :], am_ref[rows, :]], axis=1)
        else:
            rows = pl.ds(pl.multiple_of(base + at, 16), n)
            lhs = jnp.concatenate([kf_ref[rows, :], af_ref[rows, :]], axis=1)
        s = lax.dot_general(lhs, q_ref[0], NT, preferred_element_type=F32)
        s_scr[here, pl.ds(at + part * MID, n), :] = s
        return jnp.maximum(m, jnp.max(s.reshape(n // 8, 8, NQ), axis=0))

    def expo(part, at, n, m, l):
        at = pl.multiple_of(at, 16)
        p = jnp.exp(s_scr[1 - here, pl.ds(at + part * MID, n), :] - m)
        (pm_ref, pf_ref)[part][0, pl.ds(at, n), :] = p.astype(BF)
        return l + jnp.sum(p.reshape(n // 8, 8, NQ), axis=0)

    def close(m):
        m_scr[...] = jnp.broadcast_to(jnp.max(m, axis=0, keepdims=True), (8, NQ))

    def finish(l):
        linv = 1.0 / jnp.sum(l, axis=0, keepdims=True)
        linv_ref[0] = jnp.broadcast_to(linv, (8, NQ))
        turned = jnp.transpose(jnp.broadcast_to(linv, (128, NQ)))
        gs_ref[0] = (g_ref[0].astype(F32) * turned).astype(BF)

    low = jnp.full((8, NQ), -3e38, F32)
    zero = jnp.zeros((8, NQ), F32)

    @pl.when(b == 0)
    def _():
        acc[...] = jnp.zeros_like(acc)
        close(scores(1, 0, FAR, scores(0, 0, MID, low)))

    @pl.when((b > 0) & (b < NB))
    def _():
        m = m_scr[:1]
        carry = low, zero
        for part, many, parts in ((0, MID // PART, 6), (1, FAR // PART, 7)):

            def both(c, carry, part=part, parts=parts):
                fresh, l = carry
                for i in range(parts):
                    fresh = scores(part, (c * parts + i) * PART, PART, fresh)
                    l = expo(part, (c * parts + i) * PART, PART, m, l)
                return fresh, l

            carry = lax.fori_loop(0, many // parts, both, carry)
        close(carry[0])
        finish(carry[1])

    @pl.when(b == NB)
    def _():
        m, l = m_scr[:1], zero
        for part, n in ((0, MID // 2), (1, FAR // 2)):
            l = lax.fori_loop(0, 2, lambda c, l, part=part, n=n: expo(part, c * n, n, m, l), l)
        finish(l)

    @pl.when(b > 0)
    def _():
        acc[pl.ds(prior_base, FAR), :] += jnp.dot(pf_ref[0], gs_ref[0], preferred_element_type=F32)

    @pl.when(b == NB)
    def _():
        north_ref[...] = acc[:EDGE, :].astype(BF)
        south_ref[...] = acc[EDGE:, :].astype(BF)


def score_grads(p, v, gs, corr):
    gw = lax.dot_general(v, gs, NT, preferred_element_type=F32)
    return (p.astype(F32) * (gw - corr)).astype(BF)


def kernel_far(start, vm_ref, vf_ref, q_ref, gs_ref, pm_ref, pf_ref, linv_ref, o_ref, corr_ref, ds_ref, north_ref, south_ref, acc):
    b = pl.program_id(0)
    rows = pl.ds(far_base(start, b), FAR)

    @pl.when(b == 0)
    def _():
        acc[...] = jnp.zeros_like(acc)

    gs = gs_ref[0]
    ot = lax.dot_general(vm_ref[...], pm_ref[0], TN, preferred_element_type=F32)
    ot += lax.dot_general(vf_ref[rows, :], pf_ref[0], TN, preferred_element_type=F32)
    lane = lax.broadcasted_iota(jnp.int32, (NQ // 2, 128), 1)
    o = jnp.transpose(ot * linv_ref[0][:1])
    o_ref[...] = jnp.where(lane < 64, o[: NQ // 2], o[NQ // 2 :]).astype(BF)
    row = jnp.sum(gs.astype(F32) * o.astype(BF).astype(F32), axis=1, keepdims=True)
    corr = jnp.transpose(jnp.broadcast_to(row, (NQ, 128)))
    corr_ref[0] = corr[:8]
    ds = score_grads(pf_ref[0], vf_ref[rows, :], gs, corr[:1])
    ds_ref[0] = ds
    acc[rows, :] += jnp.dot(ds, q_ref[0][:, :128], preferred_element_type=F32)

    @pl.when(b == NB - 1)
    def _():
        north_ref[...] = acc[:EDGE, :].astype(BF)
        south_ref[...] = acc[EDGE:, :].astype(BF)


def kernel_mid(start, km_ref, kf_ref, vm_ref, q_ref, gs_ref, pm_ref, corr_ref, ds_ref, dq_ref, grads_ref):
    b = pl.program_id(0)

    @pl.when(b == 0)
    def _():
        grads_ref[...] = jnp.zeros_like(grads_ref)

    gs = gs_ref[0]
    ds = score_grads(pm_ref[0], vm_ref[...], gs, corr_ref[0][:1])
    grads_ref[0] += jnp.dot(ds, q_ref[0][:, :128], preferred_element_type=F32)
    dqt = lax.dot_general(km_ref[...], ds, TN, preferred_element_type=F32)
    dqt += lax.dot_general(kf_ref[pl.ds(far_base(start, b), FAR), :], ds_ref[0], TN, preferred_element_type=F32)
    grads_ref[1] += jnp.dot(pm_ref[0], gs, preferred_element_type=F32)
    lane = lax.broadcasted_iota(jnp.int32, (NQ // 2, 128), 1)
    dq = jnp.transpose(dqt * 0.125)
    dq_ref[...] = jnp.where(lane < 64, dq[: NQ // 2], dq[NQ // 2 :]).astype(BF)


def whole(*shape):
    return pl.BlockSpec(shape, lambda b, s: (0,) * len(shape))


def per_block(*shape, at=lambda b: b):
    return pl.BlockSpec((1,) + shape, lambda b, s: (at(b),) + (0,) * len(shape))


def rows_of_block():
    return pl.BlockSpec((NQ // 2, 128), lambda b, s: (b, 0))


def sds(*shape, dtype=BF):
    return jax.ShapeDtypeStruct(shape, dtype)


def call(kernel, grid, in_specs, out_specs, out_shape, scratch, flops):
    return pl.pallas_call(
        kernel,
        grid_spec=pltpu.PrefetchScalarGridSpec(
            num_scalar_prefetch=1, grid=(grid,), in_specs=in_specs, out_specs=out_specs, scratch_shapes=scratch
        ),
        out_shape=out_shape,
        compiler_params=pltpu.CompilerParams(vmem_limit_bytes=30 << 20),
        cost_estimate=pl.CostEstimate(flops=flops, bytes_accessed=14_000_000, transcendentals=0),
    )


def run_a(start, km, kf, am, af, q, g):
    ahead = lambda b: jnp.minimum(b, NB - 1)
    behind = lambda b: jnp.maximum(b - 1, 0)
    return call(
        kernel_a,
        NB + 1,
        [whole(MID, 128), whole(2 * EDGE, 128)] * 2 + [per_block(NQ, 256, at=ahead), per_block(NQ, 128, at=behind)],
        [per_block(*x, at=behind) for x in ((MID, NQ), (FAR, NQ), (8, NQ), (NQ, 128))] + [whole(EDGE, 128)] * 2,
        [sds(NB, MID, NQ), sds(NB, FAR, NQ), sds(NB, 8, NQ, dtype=F32), sds(NB, NQ, 128)] + [sds(EDGE, 128)] * 2,
        [pltpu.VMEM((2, NK, NQ), F32), pltpu.VMEM((8, NQ), F32), pltpu.VMEM((2 * EDGE, 128), F32)],
        5_000_000_000,
    )(start, km, kf, am, af, q, g)


def run_far(start, vm, vf, q, gs, pm, pf, linv):
    return call(
        kernel_far,
        NB,
        [whole(MID, 128), whole(2 * EDGE, 128), per_block(NQ, 256), per_block(NQ, 128)]
        + [per_block(MID, NQ), per_block(FAR, NQ), per_block(8, NQ)],
        [rows_of_block(), per_block(8, NQ), per_block(FAR, NQ)] + [whole(EDGE, 128)] * 2,
        [sds(T * T, 128), sds(NB, 8, NQ, dtype=F32), sds(NB, FAR, NQ)] + [sds(EDGE, 128)] * 2,
        [pltpu.VMEM((2 * EDGE, 128), F32)],
        5_000_000_000,
    )(start, vm, vf, q, gs, pm, pf, linv)


def run_mid(start, km, kf, vm, q, gs, pm, corr, ds):
    return call(
        kernel_mid,
        NB,
        [whole(MID, 128), whole(2 * EDGE, 128), whole(MID, 128), per_block(NQ, 256), per_block(NQ, 128)]
        + [per_block(MID, NQ), per_block(8, NQ), per_block(FAR, NQ)],
        [rows_of_block(), whole(2, MID, 128)],
        [sds(T * T, 128), sds(2, MID, 128, dtype=F32)],
        [],
        5_000_000_000,
    )(start, km, kf, vm, q, gs, pm, corr, ds)


def tables(first_row, height):
    i0 = first_row + BR * jnp.arange(NB, dtype=jnp.int32)
    f0 = jnp.clip(i0 - R, 0, height - 45)
    start = jnp.clip(f0 - first_row + R, 0, T - BR) // 8 * 8

    def lanes(krow, n):
        krow = krow + (first_row - R)
        kcol = lax.broadcasted_iota(jnp.int32, (n, W, 128), 1)
        lane = lax.broadcasted_iota(jnp.int32, (n, W, 128), 2)
        f = jnp.clip(first_row + lane - R, 0, height - 45)
        row_out = (lane < T) & ((krow < f) | (krow >= f + 45))
        qcol = lane - T
        col_out = (lane >= T) & (lane < 2 * T) & ((kcol < qcol + 2) | (kcol > qcol + 46))
        return jnp.where(row_out | col_out, -1e30, 0.0).astype(BF).reshape(n * W, 128)

    far = lax.broadcasted_iota(jnp.int32, (2 * R, W, 128), 0)
    mid = lax.broadcasted_iota(jnp.int32, (T, W, 128), 0) + R
    return start.astype(jnp.int32), lanes(mid, T), lanes(far + jnp.where(far >= R, T, 0), 2 * R)


def spread(x, scale):
    x = (x.reshape(NB, 1, BR * T, 128) * scale).astype(BF)
    lane = lax.broadcasted_iota(jnp.int32, (1, 2, 1, 128), 3) // 64
    head = lax.broadcasted_iota(jnp.int32, (1, 2, 1, 128), 1)
    return jnp.where(lane == head, x, jnp.zeros((), BF)).reshape(NB, NQ, 128)


def with_marks(q):
    lane = lax.broadcasted_iota(jnp.int32, (NB, 2, BR, T, 128), 4)
    row = lax.broadcasted_iota(jnp.int32, (NB, 2, BR, T, 128), 0) * BR + lax.broadcasted_iota(jnp.int32, (NB, 2, BR, T, 128), 2)
    col = lax.broadcasted_iota(jnp.int32, (NB, 2, BR, T, 128), 3)
    mark = jnp.where((lane == row) | (lane == T + col), 1.0, 0.0).astype(BF).reshape(NB, NQ, 128)
    return jnp.concatenate([spread(q, 0.125), mark], axis=2)


def shift(x, by):
    n = lax.axis_size("lat")
    return lax.ppermute(x, "lat", [(i, i + by) for i in range(n) if 0 <= i + by < n])


def swap(x, first):
    n = lax.axis_size("lon")
    pairs = [(i % n, (i + 1) % n) for i in range(first, n + first, 2)]
    return lax.ppermute(x, "lon", pairs + [(b, a) for a, b in pairs])


def far_rows(mid):
    return jnp.concatenate([shift(mid[T - R :], 1), shift(mid[:R], -1)], axis=0).reshape(2 * EDGE, 128)


def from_lat(north, south):
    from_south = shift(north, -1).reshape(R, W, 128).astype(F32)
    from_north = shift(south, 1).reshape(R, W, 128).astype(F32)
    pad = ((T - R, 0), (0, 0), (0, 0)), ((0, T - R), (0, 0), (0, 0))
    return jnp.pad(from_south, pad[0]) + jnp.pad(from_north, pad[1])


def body(queries, keys, values, out_grad):
    height = T * lax.axis_size("lat")
    even = lax.axis_index("lon") % 2 == 0
    start, am, af = tables(lax.axis_index("lat") * T, height)
    q = with_marks(queries)
    g = spread(out_grad, 1.0)
    pair = jnp.stack([keys, values])
    near, far = swap(pair, 0), swap(pair, 1)

    def widen(x, i):
        return jnp.concatenate([jnp.where(even, far[i], near[i]), x, jnp.where(even, near[i], far[i])], axis=1)

    km = widen(keys, 0)
    vm = widen(values, 1)
    kf = far_rows(km)
    vf = far_rows(vm)
    km = km.reshape(MID, 128)
    vm = vm.reshape(MID, 128)
    pm, pf, linv, gs, *dvf = run_a(start, km, kf, am, af, q, g)
    dvf = from_lat(*dvf)
    attended, corr, ds, *dkf = run_far(start, vm, vf, q, gs, pm, pf, linv)
    dkf = from_lat(*dkf)
    grad_queries, mid = run_mid(start, km, kf, vm, q, gs, pm, corr, ds)
    mid = mid.reshape(2, T, W, 128) + jnp.stack([dkf, dvf])
    west = mid[:, :, :T].astype(BF)
    east = mid[:, :, 2 * T :].astype(BF)
    near = swap(jnp.where(even, east, west), 0)
    far = swap(jnp.where(even, west, east), 1)
    grads = [(mid[i, :, T : 2 * T] + near[i].astype(F32) + far[i].astype(F32)).astype(BF) for i in range(2)]
    return attended.reshape(T, T, 128), grad_queries.reshape(T, T, 128), grads[0], grads[1]


def solution(mesh):
    spec = P("lat", "lon", None)
    return jax.shard_map(body, mesh=mesh, in_specs=(spec,) * 4, out_specs=(spec,) * 4, check_vma=False)
```

```python
import jax
import jax.numpy as jnp
from jax import lax
from jax.experimental import pallas as pl
from jax.experimental.pallas import tpu as pltpu
from jax.sharding import PartitionSpec as P


R = 22
T = 24
W = 3 * T
BR = 8
NB = T // BR
SR = BR + 2 * R
NQ = 2 * BR * T
MID = T * W
EDGE = R * W
FAR = (SR - T) * W
PART = 2 * W
F32 = jnp.float32
BF = jnp.bfloat16
NT = (((1,), (1,)), ((), ()))
TN = (((0,), (0,)), ((), ()))


def far_base(start, b):
    return pl.multiple_of(start[b] * W, 64)


def kernel_early(start, km_ref, am_ref, q_ref, s_ref, m_ref):
    lhs = jnp.concatenate([km_ref[...], am_ref[...]], axis=1)
    s = lax.dot_general(lhs, q_ref[0], NT, preferred_element_type=F32)
    s_ref[0] = s
    m_ref[0] = jnp.max(s.reshape(MID // 8, 8, NQ), axis=0)


def kernel_a(start, kf_ref, af_ref, q_ref, g_ref, sm_ref, mm_ref, pm_ref, pf_ref, linv_ref, gs_ref, north_ref, south_ref, s_scr, m_scr, acc):
    b = pl.program_id(0)
    here = lax.rem(b, 2)
    base = far_base(start, jnp.minimum(b, NB - 1))
    prior_base = far_base(start, jnp.maximum(b - 1, 0))

    def scores(at, n, m):
        rows = pl.ds(pl.multiple_of(base + at, 16), n)
        lhs = jnp.concatenate([kf_ref[rows, :], af_ref[rows, :]], axis=1)
        s = lax.dot_general(lhs, q_ref[0], NT, preferred_element_type=F32)
        s_scr[here, pl.ds(pl.multiple_of(at, 16), n), :] = s
        return jnp.maximum(m, jnp.max(s.reshape(n // 8, 8, NQ), axis=0))

    def expo(s, p_ref, at, n, m, l):
        p = jnp.exp(s - m)
        p_ref[0, pl.ds(at, n), :] = p.astype(BF)
        return l + jnp.sum(p.reshape(n // 8, 8, NQ), axis=0)

    def expo_mid(c, l):
        at = pl.multiple_of(c * (MID // 2), 16)
        return expo(sm_ref[0, pl.ds(at, MID // 2), :], pm_ref, at, MID // 2, m_scr[:1], l)

    def expo_far(at, n, m, l):
        at = pl.multiple_of(at, 16)
        return expo(s_scr[1 - here, pl.ds(at, n), :], pf_ref, at, n, m, l)

    def close(m):
        m_scr[...] = jnp.broadcast_to(jnp.max(m, axis=0, keepdims=True), (8, NQ))

    def finish(l):
        linv = 1.0 / jnp.sum(l, axis=0, keepdims=True)
        linv_ref[0] = jnp.broadcast_to(linv, (8, NQ))
        turned = jnp.transpose(jnp.broadcast_to(linv, (128, NQ)))
        gs_ref[0] = (g_ref[0].astype(F32) * turned).astype(BF)

    zero = jnp.zeros((8, NQ), F32)

    @pl.when(b == 0)
    def _():
        acc[...] = jnp.zeros_like(acc)
        close(scores(0, FAR, mm_ref[0]))

    @pl.when((b > 0) & (b < NB))
    def _():
        m = m_scr[:1]
        l = lax.fori_loop(0, 2, expo_mid, zero)

        def both(c, carry):
            fresh, l = carry
            for i in range(7):
                fresh = scores((c * 7 + i) * PART, PART, fresh)
                l = expo_far((c * 7 + i) * PART, PART, m, l)
            return fresh, l

        fresh, l = lax.fori_loop(0, 2, both, (mm_ref[0], l))
        close(fresh)
        finish(l)

    @pl.when(b == NB)
    def _():
        m = m_scr[:1]
        l = lax.fori_loop(0, 2, expo_mid, zero)
        finish(lax.fori_loop(0, 2, lambda c, l: expo_far(c * (FAR // 2), FAR // 2, m, l), l))

    @pl.when(b > 0)
    def _():
        acc[pl.ds(prior_base, FAR), :] += jnp.dot(pf_ref[0], gs_ref[0], preferred_element_type=F32)

    @pl.when(b == NB)
    def _():
        north_ref[...] = acc[:EDGE, :].astype(BF)
        south_ref[...] = acc[EDGE:, :].astype(BF)


def score_grads(p, v, gs, corr):
    gw = lax.dot_general(v, gs, NT, preferred_element_type=F32)
    return (p.astype(F32) * (gw - corr)).astype(BF)


def kernel_far(start, vm_ref, vf_ref, q_ref, gs_ref, pm_ref, pf_ref, linv_ref, o_ref, corr_ref, ds_ref, north_ref, south_ref, acc):
    b = pl.program_id(0)
    rows = pl.ds(far_base(start, b), FAR)

    @pl.when(b == 0)
    def _():
        acc[...] = jnp.zeros_like(acc)

    gs = gs_ref[0]
    ot = lax.dot_general(vm_ref[...], pm_ref[0], TN, preferred_element_type=F32)
    ot += lax.dot_general(vf_ref[rows, :], pf_ref[0], TN, preferred_element_type=F32)
    lane = lax.broadcasted_iota(jnp.int32, (NQ // 2, 128), 1)
    o = jnp.transpose(ot * linv_ref[0][:1])
    o_ref[...] = jnp.where(lane < 64, o[: NQ // 2], o[NQ // 2 :]).astype(BF)
    row = jnp.sum(gs.astype(F32) * o.astype(BF).astype(F32), axis=1, keepdims=True)
    corr = jnp.transpose(jnp.broadcast_to(row, (NQ, 128)))
    corr_ref[0] = corr[:8]
    ds = score_grads(pf_ref[0], vf_ref[rows, :], gs, corr[:1])
    ds_ref[0] = ds
    acc[rows, :] += jnp.dot(ds, q_ref[0][:, :128], preferred_element_type=F32)

    @pl.when(b == NB - 1)
    def _():
        north_ref[...] = acc[:EDGE, :].astype(BF)
        south_ref[...] = acc[EDGE:, :].astype(BF)


def kernel_mid(start, km_ref, kf_ref, vm_ref, q_ref, gs_ref, pm_ref, corr_ref, ds_ref, dq_ref, grads_ref):
    b = pl.program_id(0)

    @pl.when(b == 0)
    def _():
        grads_ref[...] = jnp.zeros_like(grads_ref)

    gs = gs_ref[0]
    ds = score_grads(pm_ref[0], vm_ref[...], gs, corr_ref[0][:1])
    grads_ref[0] += jnp.dot(ds, q_ref[0][:, :128], preferred_element_type=F32)
    dqt = lax.dot_general(km_ref[...], ds, TN, preferred_element_type=F32)
    dqt += lax.dot_general(kf_ref[pl.ds(far_base(start, b), FAR), :], ds_ref[0], TN, preferred_element_type=F32)
    grads_ref[1] += jnp.dot(pm_ref[0], gs, preferred_element_type=F32)
    lane = lax.broadcasted_iota(jnp.int32, (NQ // 2, 128), 1)
    dq = jnp.transpose(dqt * 0.125)
    dq_ref[...] = jnp.where(lane < 64, dq[: NQ // 2], dq[NQ // 2 :]).astype(BF)


def whole(*shape):
    return pl.BlockSpec(shape, lambda b, s: (0,) * len(shape))


def per_block(*shape, at=lambda b: b):
    return pl.BlockSpec((1,) + shape, lambda b, s: (at(b),) + (0,) * len(shape))


def rows_of_block():
    return pl.BlockSpec((NQ // 2, 128), lambda b, s: (b, 0))


def sds(*shape, dtype=BF):
    return jax.ShapeDtypeStruct(shape, dtype)


def call(kernel, grid, in_specs, out_specs, out_shape, scratch, flops):
    return pl.pallas_call(
        kernel,
        grid_spec=pltpu.PrefetchScalarGridSpec(
            num_scalar_prefetch=1, grid=(grid,), in_specs=in_specs, out_specs=out_specs, scratch_shapes=scratch
        ),
        out_shape=out_shape,
        compiler_params=pltpu.CompilerParams(vmem_limit_bytes=24 << 20),
        cost_estimate=pl.CostEstimate(flops=flops, bytes_accessed=14_000_000, transcendentals=0),
    )


def run_early(start, km, am, q):
    return call(
        kernel_early,
        NB,
        [whole(MID, 128), whole(MID, 128), per_block(NQ, 256)],
        [per_block(MID, NQ), per_block(8, NQ)],
        [sds(NB, MID, NQ, dtype=F32), sds(NB, 8, NQ, dtype=F32)],
        [],
        1_000_000_000,
    )(start, km, am, q)


def run_a(start, kf, af, q, g, sm, mm):
    ahead = lambda b: jnp.minimum(b, NB - 1)
    behind = lambda b: jnp.maximum(b - 1, 0)
    return call(
        kernel_a,
        NB + 1,
        [whole(2 * EDGE, 128), whole(2 * EDGE, 128), per_block(NQ, 256, at=ahead), per_block(NQ, 128, at=behind)]
        + [per_block(MID, NQ, at=behind), per_block(8, NQ, at=ahead)],
        [per_block(*x, at=behind) for x in ((MID, NQ), (FAR, NQ), (8, NQ), (NQ, 128))] + [whole(EDGE, 128)] * 2,
        [sds(NB, MID, NQ), sds(NB, FAR, NQ), sds(NB, 8, NQ, dtype=F32), sds(NB, NQ, 128)] + [sds(EDGE, 128)] * 2,
        [pltpu.VMEM((2, FAR, NQ), F32), pltpu.VMEM((8, NQ), F32), pltpu.VMEM((2 * EDGE, 128), F32)],
        5_000_000_000,
    )(start, kf, af, q, g, sm, mm)


def run_far(start, vm, vf, q, gs, pm, pf, linv):
    return call(
        kernel_far,
        NB,
        [whole(MID, 128), whole(2 * EDGE, 128), per_block(NQ, 256), per_block(NQ, 128)]
        + [per_block(MID, NQ), per_block(FAR, NQ), per_block(8, NQ)],
        [rows_of_block(), per_block(8, NQ), per_block(FAR, NQ)] + [whole(EDGE, 128)] * 2,
        [sds(T * T, 128), sds(NB, 8, NQ, dtype=F32), sds(NB, FAR, NQ)] + [sds(EDGE, 128)] * 2,
        [pltpu.VMEM((2 * EDGE, 128), F32)],
        5_000_000_000,
    )(start, vm, vf, q, gs, pm, pf, linv)


def run_mid(start, km, kf, vm, q, gs, pm, corr, ds):
    return call(
        kernel_mid,
        NB,
        [whole(MID, 128), whole(2 * EDGE, 128), whole(MID, 128), per_block(NQ, 256), per_block(NQ, 128)]
        + [per_block(MID, NQ), per_block(8, NQ), per_block(FAR, NQ)],
        [rows_of_block(), whole(2, MID, 128)],
        [sds(T * T, 128), sds(2, MID, 128, dtype=F32)],
        [],
        5_000_000_000,
    )(start, km, kf, vm, q, gs, pm, corr, ds)


def tables(first_row, height):
    i0 = first_row + BR * jnp.arange(NB, dtype=jnp.int32)
    f0 = jnp.clip(i0 - R, 0, height - 45)
    start = jnp.clip(f0 - first_row + R, 0, T - BR) // 8 * 8

    def lanes(krow, n):
        krow = krow + (first_row - R)
        kcol = lax.broadcasted_iota(jnp.int32, (n, W, 128), 1)
        lane = lax.broadcasted_iota(jnp.int32, (n, W, 128), 2)
        f = jnp.clip(first_row + lane - R, 0, height - 45)
        row_out = (lane < T) & ((krow < f) | (krow >= f + 45))
        qcol = lane - T
        col_out = (lane >= T) & (lane < 2 * T) & ((kcol < qcol + 2) | (kcol > qcol + 46))
        return jnp.where(row_out | col_out, -1e30, 0.0).astype(BF).reshape(n * W, 128)

    far = lax.broadcasted_iota(jnp.int32, (2 * R, W, 128), 0)
    mid = lax.broadcasted_iota(jnp.int32, (T, W, 128), 0) + R
    return start.astype(jnp.int32), lanes(mid, T), lanes(far + jnp.where(far >= R, T, 0), 2 * R)


def spread(x, scale):
    x = (x.reshape(NB, 1, BR * T, 128) * scale).astype(BF)
    lane = lax.broadcasted_iota(jnp.int32, (1, 2, 1, 128), 3) // 64
    head = lax.broadcasted_iota(jnp.int32, (1, 2, 1, 128), 1)
    return jnp.where(lane == head, x, jnp.zeros((), BF)).reshape(NB, NQ, 128)


def with_marks(q):
    lane = lax.broadcasted_iota(jnp.int32, (NB, 2, BR, T, 128), 4)
    row = lax.broadcasted_iota(jnp.int32, (NB, 2, BR, T, 128), 0) * BR + lax.broadcasted_iota(jnp.int32, (NB, 2, BR, T, 128), 2)
    col = lax.broadcasted_iota(jnp.int32, (NB, 2, BR, T, 128), 3)
    mark = jnp.where((lane == row) | (lane == T + col), 1.0, 0.0).astype(BF).reshape(NB, NQ, 128)
    return jnp.concatenate([spread(q, 0.125), mark], axis=2)


def shift(x, by):
    n = lax.axis_size("lat")
    return lax.ppermute(x, "lat", [(i, i + by) for i in range(n) if 0 <= i + by < n])


def swap(x, first):
    n = lax.axis_size("lon")
    pairs = [(i % n, (i + 1) % n) for i in range(first, n + first, 2)]
    return lax.ppermute(x, "lon", pairs + [(b, a) for a, b in pairs])


def far_rows(mid):
    return jnp.concatenate([shift(mid[T - R :], 1), shift(mid[:R], -1)], axis=0).reshape(2 * EDGE, 128)


def from_lat(north, south):
    from_south = shift(north, -1).reshape(R, W, 128).astype(F32)
    from_north = shift(south, 1).reshape(R, W, 128).astype(F32)
    pad = ((T - R, 0), (0, 0), (0, 0)), ((0, T - R), (0, 0), (0, 0))
    return jnp.pad(from_south, pad[0]) + jnp.pad(from_north, pad[1])


def body(queries, keys, values, out_grad):
    height = T * lax.axis_size("lat")
    even = lax.axis_index("lon") % 2 == 0
    start, am, af = tables(lax.axis_index("lat") * T, height)
    q = with_marks(queries)
    g = spread(out_grad, 1.0)
    pair = jnp.stack([keys, values])
    near = swap(pair, 0)
    far = swap(pair, 1)

    def widen(x, i):
        return jnp.concatenate([jnp.where(even, far[i], near[i]), x, jnp.where(even, near[i], far[i])], axis=1)

    km = widen(keys, 0)
    vm = widen(values, 1)
    kf = far_rows(km)
    vf = far_rows(vm)
    km = km.reshape(MID, 128)
    vm = vm.reshape(MID, 128)
    sm, mm = run_early(start, km, am, q)
    pm, pf, linv, gs, *dvf = run_a(start, kf, af, q, g, sm, mm)
    dvf = from_lat(*dvf)
    attended, corr, ds, *dkf = run_far(start, vm, vf, q, gs, pm, pf, linv)
    dkf = from_lat(*dkf)
    grad_queries, mid = run_mid(start, km, kf, vm, q, gs, pm, corr, ds)
    mid = mid.reshape(2, T, W, 128) + jnp.stack([dkf, dvf])
    west = mid[:, :, :T].astype(BF)
    east = mid[:, :, 2 * T :].astype(BF)
    near = swap(jnp.where(even, east, west), 0)
    far = swap(jnp.where(even, west, east), 1)
    grads = [(mid[i, :, T : 2 * T] + near[i].astype(F32) + far[i].astype(F32)).astype(BF) for i in range(2)]
    return attended.reshape(T, T, 128), grad_queries.reshape(T, T, 128), grads[0], grads[1]


def solution(mesh):
    spec = P("lat", "lon", None)
    return jax.shard_map(body, mesh=mesh, in_specs=(spec,) * 4, out_specs=(spec,) * 4, check_vma=False)
```

```python
import jax
import jax.numpy as jnp
from jax import lax
from jax.experimental import pallas as pl
from jax.experimental.pallas import tpu as pltpu
from jax.sharding import PartitionSpec as P


R = 22
T = 24
W = 3 * T
BR = 8
NB = T // BR
SR = BR + 2 * R
NQ = 2 * BR * T
MID = T * W
EDGE = R * W
FAR = (SR - T) * W
PART = 2 * W
F32 = jnp.float32
BF = jnp.bfloat16
NT = (((1,), (1,)), ((), ()))
TN = (((0,), (0,)), ((), ()))


def far_base(start, b):
    return pl.multiple_of(start[b] * W, 64)


def kernel_early(start, km_ref, am_ref, q_ref, s_ref, m_ref):
    lhs = jnp.concatenate([km_ref[...], am_ref[...]], axis=1)
    s = lax.dot_general(lhs, q_ref[0], NT, preferred_element_type=F32)
    s_ref[0] = s
    m_ref[0] = jnp.max(s.reshape(MID // 8, 8, NQ), axis=0)


def kernel_a(start, kf_ref, af_ref, q_ref, g_ref, sm_ref, mm_ref, pm_ref, pf_ref, linv_ref, gs_ref, north_ref, south_ref, s_scr, m_scr, acc):
    b = pl.program_id(0)
    here = lax.rem(b, 2)
    base = far_base(start, jnp.minimum(b, NB - 1))
    prior_base = far_base(start, jnp.maximum(b - 1, 0))

    def scores(at, n, m):
        rows = pl.ds(pl.multiple_of(base + at, 16), n)
        lhs = jnp.concatenate([kf_ref[rows, :], af_ref[rows, :]], axis=1)
        s = lax.dot_general(lhs, q_ref[0], NT, preferred_element_type=F32)
        s_scr[here, pl.ds(pl.multiple_of(at, 16), n), :] = s
        return jnp.maximum(m, jnp.max(s.reshape(n // 8, 8, NQ), axis=0))

    def expo(s, p_ref, at, n, m, l):
        p = jnp.exp(s - m)
        p_ref[0, pl.ds(at, n), :] = p.astype(BF)
        return l + jnp.sum(p.reshape(n // 8, 8, NQ), axis=0)

    def expo_mid(c, l):
        at = pl.multiple_of(c * (MID // 2), 16)
        return expo(sm_ref[0, pl.ds(at, MID // 2), :], pm_ref, at, MID // 2, m_scr[:1], l)

    def expo_far(at, n, m, l):
        at = pl.multiple_of(at, 16)
        return expo(s_scr[1 - here, pl.ds(at, n), :], pf_ref, at, n, m, l)

    def close(m):
        m_scr[...] = jnp.broadcast_to(jnp.max(m, axis=0, keepdims=True), (8, NQ))

    def finish(l):
        linv = 1.0 / jnp.sum(l, axis=0, keepdims=True)
        linv_ref[0] = jnp.broadcast_to(linv, (8, NQ))
        turned = jnp.transpose(jnp.broadcast_to(linv, (128, NQ)))
        gs_ref[0] = (g_ref[0].astype(F32) * turned).astype(BF)

    zero = jnp.zeros((8, NQ), F32)

    @pl.when(b == 0)
    def _():
        acc[...] = jnp.zeros_like(acc)
        close(scores(0, FAR, mm_ref[0]))

    @pl.when((b > 0) & (b < NB))
    def _():
        m = m_scr[:1]
        l = lax.fori_loop(0, 2, expo_mid, zero)

        def both(c, carry):
            fresh, l = carry
            for i in range(7):
                fresh = scores((c * 7 + i) * PART, PART, fresh)
                l = expo_far((c * 7 + i) * PART, PART, m, l)
            return fresh, l

        fresh, l = lax.fori_loop(0, 2, both, (mm_ref[0], l))
        close(fresh)
        finish(l)

    @pl.when(b == NB)
    def _():
        m = m_scr[:1]
        l = lax.fori_loop(0, 2, expo_mid, zero)
        finish(lax.fori_loop(0, 2, lambda c, l: expo_far(c * (FAR // 2), FAR // 2, m, l), l))

    @pl.when(b > 0)
    def _():
        acc[pl.ds(prior_base, FAR), :] += jnp.dot(pf_ref[0], gs_ref[0], preferred_element_type=F32)

    @pl.when(b == NB)
    def _():
        north_ref[...] = acc[:EDGE, :].astype(BF)
        south_ref[...] = acc[EDGE:, :].astype(BF)


def score_grads(p, v, gs, corr):
    gw = lax.dot_general(v, gs, NT, preferred_element_type=F32)
    return (p.astype(F32) * (gw - corr)).astype(BF)


def kernel_far(start, vm_ref, vf_ref, q_ref, gs_ref, pm_ref, pf_ref, linv_ref, o_ref, corr_ref, ds_ref, north_ref, south_ref, acc):
    b = pl.program_id(0)
    rows = pl.ds(far_base(start, b), FAR)

    @pl.when(b == 0)
    def _():
        acc[...] = jnp.zeros_like(acc)

    gs = gs_ref[0]
    ot = lax.dot_general(vm_ref[...], pm_ref[0], TN, preferred_element_type=F32)
    ot += lax.dot_general(vf_ref[rows, :], pf_ref[0], TN, preferred_element_type=F32)
    lane = lax.broadcasted_iota(jnp.int32, (NQ // 2, 128), 1)
    o = jnp.transpose(ot * linv_ref[0][:1])
    o_ref[...] = jnp.where(lane < 64, o[: NQ // 2], o[NQ // 2 :]).astype(BF)
    row = jnp.sum(gs.astype(F32) * o.astype(BF).astype(F32), axis=1, keepdims=True)
    corr = jnp.transpose(jnp.broadcast_to(row, (NQ, 128)))
    corr_ref[0] = corr[:8]
    ds = score_grads(pf_ref[0], vf_ref[rows, :], gs, corr[:1])
    ds_ref[0] = ds
    acc[rows, :] += jnp.dot(ds, q_ref[0][:, :128], preferred_element_type=F32)

    @pl.when(b == NB - 1)
    def _():
        north_ref[...] = acc[:EDGE, :].astype(BF)
        south_ref[...] = acc[EDGE:, :].astype(BF)


def kernel_mid(start, km_ref, kf_ref, vm_ref, q_ref, gs_ref, pm_ref, corr_ref, ds_ref, dq_ref, grads_ref):
    b = pl.program_id(0)

    @pl.when(b == 0)
    def _():
        grads_ref[...] = jnp.zeros_like(grads_ref)

    gs = gs_ref[0]
    ds = score_grads(pm_ref[0], vm_ref[...], gs, corr_ref[0][:1])
    grads_ref[0] += jnp.dot(ds, q_ref[0][:, :128], preferred_element_type=F32)
    dqt = lax.dot_general(km_ref[...], ds, TN, preferred_element_type=F32)
    dqt += lax.dot_general(kf_ref[pl.ds(far_base(start, b), FAR), :], ds_ref[0], TN, preferred_element_type=F32)
    grads_ref[1] += jnp.dot(pm_ref[0], gs, preferred_element_type=F32)
    lane = lax.broadcasted_iota(jnp.int32, (NQ // 2, 128), 1)
    dq = jnp.transpose(dqt * 0.125)
    dq_ref[...] = jnp.where(lane < 64, dq[: NQ // 2], dq[NQ // 2 :]).astype(BF)


def whole(*shape):
    return pl.BlockSpec(shape, lambda b, s: (0,) * len(shape))


def per_block(*shape, at=lambda b: b):
    return pl.BlockSpec((1,) + shape, lambda b, s: (at(b),) + (0,) * len(shape))


def rows_of_block():
    return pl.BlockSpec((NQ // 2, 128), lambda b, s: (b, 0))


def sds(*shape, dtype=BF):
    return jax.ShapeDtypeStruct(shape, dtype)


def call(kernel, grid, in_specs, out_specs, out_shape, scratch, flops):
    return pl.pallas_call(
        kernel,
        grid_spec=pltpu.PrefetchScalarGridSpec(
            num_scalar_prefetch=1, grid=(grid,), in_specs=in_specs, out_specs=out_specs, scratch_shapes=scratch
        ),
        out_shape=out_shape,
        compiler_params=pltpu.CompilerParams(vmem_limit_bytes=24 << 20),
        cost_estimate=pl.CostEstimate(flops=flops, bytes_accessed=14_000_000, transcendentals=0),
    )


def run_early(start, km, am, q):
    return call(
        kernel_early,
        NB,
        [whole(MID, 128), whole(MID, 128), per_block(NQ, 256)],
        [per_block(MID, NQ), per_block(8, NQ)],
        [sds(NB, MID, NQ, dtype=F32), sds(NB, 8, NQ, dtype=F32)],
        [],
        1_000_000_000,
    )(start, km, am, q)


def run_a(start, kf, af, q, g, sm, mm):
    ahead = lambda b: jnp.minimum(b, NB - 1)
    behind = lambda b: jnp.maximum(b - 1, 0)
    return call(
        kernel_a,
        NB + 1,
        [whole(2 * EDGE, 128), whole(2 * EDGE, 128), per_block(NQ, 256, at=ahead), per_block(NQ, 128, at=behind)]
        + [per_block(MID, NQ, at=behind), per_block(8, NQ, at=ahead)],
        [per_block(*x, at=behind) for x in ((MID, NQ), (FAR, NQ), (8, NQ), (NQ, 128))] + [whole(EDGE, 128)] * 2,
        [sds(NB, MID, NQ), sds(NB, FAR, NQ), sds(NB, 8, NQ, dtype=F32), sds(NB, NQ, 128)] + [sds(EDGE, 128)] * 2,
        [pltpu.VMEM((2, FAR, NQ), F32), pltpu.VMEM((8, NQ), F32), pltpu.VMEM((2 * EDGE, 128), F32)],
        5_000_000_000,
    )(start, kf, af, q, g, sm, mm)


def run_far(start, vm, vf, q, gs, pm, pf, linv):
    return call(
        kernel_far,
        NB,
        [whole(MID, 128), whole(2 * EDGE, 128), per_block(NQ, 256), per_block(NQ, 128)]
        + [per_block(MID, NQ), per_block(FAR, NQ), per_block(8, NQ)],
        [rows_of_block(), per_block(8, NQ), per_block(FAR, NQ)] + [whole(EDGE, 128)] * 2,
        [sds(T * T, 128), sds(NB, 8, NQ, dtype=F32), sds(NB, FAR, NQ)] + [sds(EDGE, 128)] * 2,
        [pltpu.VMEM((2 * EDGE, 128), F32)],
        5_000_000_000,
    )(start, vm, vf, q, gs, pm, pf, linv)


def run_mid(start, km, kf, vm, q, gs, pm, corr, ds):
    return call(
        kernel_mid,
        NB,
        [whole(MID, 128), whole(2 * EDGE, 128), whole(MID, 128), per_block(NQ, 256), per_block(NQ, 128)]
        + [per_block(MID, NQ), per_block(8, NQ), per_block(FAR, NQ)],
        [rows_of_block(), whole(2, MID, 128)],
        [sds(T * T, 128), sds(2, MID, 128, dtype=F32)],
        [],
        5_000_000_000,
    )(start, km, kf, vm, q, gs, pm, corr, ds)


def tables(first_row, height):
    i0 = first_row + BR * jnp.arange(NB, dtype=jnp.int32)
    f0 = jnp.clip(i0 - R, 0, height - 45)
    start = jnp.clip(f0 - first_row + R, 0, T - BR) // 8 * 8

    def lanes(krow, n):
        krow = krow + (first_row - R)
        kcol = lax.broadcasted_iota(jnp.int32, (n, W, 128), 1)
        lane = lax.broadcasted_iota(jnp.int32, (n, W, 128), 2)
        f = jnp.clip(first_row + lane - R, 0, height - 45)
        row_out = (lane < T) & ((krow < f) | (krow >= f + 45))
        qcol = lane - T
        col_out = (lane >= T) & (lane < 2 * T) & ((kcol < qcol + 2) | (kcol > qcol + 46))
        return jnp.where(row_out | col_out, -1e30, 0.0).astype(BF).reshape(n * W, 128)

    far = lax.broadcasted_iota(jnp.int32, (2 * R, W, 128), 0)
    mid = lax.broadcasted_iota(jnp.int32, (T, W, 128), 0) + R
    return start.astype(jnp.int32), lanes(mid, T), lanes(far + jnp.where(far >= R, T, 0), 2 * R)


def spread(x, scale):
    x = (x.reshape(NB, 1, BR * T, 128) * scale).astype(BF)
    lane = lax.broadcasted_iota(jnp.int32, (1, 2, 1, 128), 3) // 64
    head = lax.broadcasted_iota(jnp.int32, (1, 2, 1, 128), 1)
    return jnp.where(lane == head, x, jnp.zeros((), BF)).reshape(NB, NQ, 128)


def with_marks(q):
    lane = lax.broadcasted_iota(jnp.int32, (NB, 2, BR, T, 128), 4)
    row = lax.broadcasted_iota(jnp.int32, (NB, 2, BR, T, 128), 0) * BR + lax.broadcasted_iota(jnp.int32, (NB, 2, BR, T, 128), 2)
    col = lax.broadcasted_iota(jnp.int32, (NB, 2, BR, T, 128), 3)
    mark = jnp.where((lane == row) | (lane == T + col), 1.0, 0.0).astype(BF).reshape(NB, NQ, 128)
    return jnp.concatenate([spread(q, 0.125), mark], axis=2)


def shift(x, by):
    n = lax.axis_size("lat")
    return lax.ppermute(x, "lat", [(i, i + by) for i in range(n) if 0 <= i + by < n])


def swap(x, first):
    n = lax.axis_size("lon")
    pairs = [(i % n, (i + 1) % n) for i in range(first, n + first, 2)]
    return lax.ppermute(x, "lon", pairs + [(b, a) for a, b in pairs])


def far_rows(mid):
    return jnp.concatenate([shift(mid[T - R :], 1), shift(mid[:R], -1)], axis=0).reshape(2 * EDGE, 128)


def from_lat(north, south):
    from_south = shift(north, -1).reshape(R, W, 128).astype(F32)
    from_north = shift(south, 1).reshape(R, W, 128).astype(F32)
    pad = ((T - R, 0), (0, 0), (0, 0)), ((0, T - R), (0, 0), (0, 0))
    return jnp.pad(from_south, pad[0]) + jnp.pad(from_north, pad[1])


def body(queries, keys, values, out_grad):
    height = T * lax.axis_size("lat")
    even = lax.axis_index("lon") % 2 == 0
    start, am, af = tables(lax.axis_index("lat") * T, height)
    q = with_marks(queries)
    g = spread(out_grad, 1.0)
    pair = jnp.stack([keys, values])
    near = swap(pair, 0)
    far = swap(pair, 1)

    def widen(x, i):
        return jnp.concatenate([jnp.where(even, far[i], near[i]), x, jnp.where(even, near[i], far[i])], axis=1)

    km = widen(keys, 0)
    vm = widen(values, 1)
    kf = far_rows(km)
    vf = far_rows(vm)
    km = km.reshape(MID, 128)
    vm = vm.reshape(MID, 128)
    sm, mm = run_early(start, km, am, q)
    pm, pf, linv, gs, *dvf = run_a(start, kf, af, q, g, sm, mm)
    dvf = from_lat(*dvf)
    attended, corr, ds, *dkf = run_far(start, vm, vf, q, gs, pm, pf, linv)
    dkf = from_lat(*dkf)
    grad_queries, mid = run_mid(start, km, kf, vm, q, gs, pm, corr, ds)
    mid = mid.reshape(2, T, W, 128)

    def fold_lon(x):
        west = x[:, :T].astype(BF)
        east = x[:, 2 * T :].astype(BF)
        near = swap(jnp.where(even, east, west), 0)
        far = swap(jnp.where(even, west, east), 1)
        return (x[:, T : 2 * T] + near.astype(F32) + far.astype(F32)).astype(BF)

    grad_values = fold_lon(mid[1] + dvf)
    grad_keys = fold_lon(mid[0] + dkf)
    return attended.reshape(T, T, 128), grad_queries.reshape(T, T, 128), grad_keys, grad_values


def solution(mesh):
    spec = P("lat", "lon", None)
    return jax.shard_map(body, mesh=mesh, in_specs=(spec,) * 4, out_specs=(spec,) * 4, check_vma=False)
```
